128 devices in a mesh: section: 2 (over x_hi), dp: 8 (over z, core), mp: 8 (over x_lo, y).
Axes of the slice: x: 4 (x_hi: 2, x_lo: 2; x = x_hi * 2 + x_lo), y: 4, z: 4, core: 2. Of those that a mesh axis runs over, the one named last changes fastest.
Arguments:
- inputs: bfloat16 [2, 16, 128, 4096], P('section', 'dp'), may hold values from -6 to 6
- norm_gains: bfloat16 [2, 4096], P('section'), may hold values from 0.5 to 1.5
- weights: bfloat16 [2, 4096, 4, 4096], P('section', 'dp', None, 'mp'), may hold values from -0.09375 to 0.09375
- cotangent: bfloat16 [16, 128, 4096], P('dp'), may hold values from -6 to 6
- lengths: int32 [2, 16], P(None, 'dp'), may hold values from 32 to 128, as said below
- dp_noise: float32 [2, 4096, 4, 4096], P('section', 'dp', None, 'mp'), may hold values from -6 to 6
Outputs:
- noisy_grad: float32 [2, 4096, 4, 4096], P('section', 'dp', None, 'mp')
- clip_scale: float32 [16], P('dp')
The draws below stay inside these ranges and needn't reach their ends.
Inputs may be any that keep to these rules, and one draw needn't show every extreme that they name: `lengths`: the first example of each row has length 128.
All inputs are finite; a program needn't handle non-finite values.
Results may differ from the reference program's by a relative error of at most 0.024.
Values may be sent and summed in bfloat16 or wider, within the bound.
A program may use at most 256 MiB of HBM per device.

```python
import jax
import jax.numpy as jnp
from jax import lax

D = 4096
HEAD = 64
S = 128
MB = 2
INNER = 4096
EXAMPLES = 16
N_DP = 8
N_MP = 8


def draw_lengths(key, part):
    drawn = jax.random.randint(key, (2, EXAMPLES), S // 4, S + 1, dtype=jnp.int32)
    column = jnp.arange(EXAMPLES)[None, :]
    return jnp.where(column == 0, S, drawn).astype(jnp.int32)


def block_scale(rng, dims, split, least, largest):
    gain = 1.0
    for dim, parts in split:
        heights = jax.random.uniform(jax.random.fold_in(jax.random.fold_in(rng, 6), dim), (parts,), jnp.float32, least / len(split), largest / len(split))
        gain = gain * jnp.repeat(jnp.exp(heights), dims[dim] // parts).reshape((-1,) + (1,) * (len(dims) - 1 - dim))
    return gain


def noise(rng, extent, spread, most, cuts=(), kind=jnp.bfloat16):
    values = spread * jax.random.normal(rng, extent, jnp.float32)
    if cuts:
        values = values * block_scale(rng, extent, cuts, -0.22, 0.18)
    return jnp.clip(values, -most, most).astype(kind)


def setup_inputs(seed: int = 0) -> dict:
    streams_of = jax.random.split(jax.random.key(seed), 7)
    return {
        "inputs": noise(streams_of[0], (2, EXAMPLES, S, D), 1.0, 6.0, ((0, 2), (1, 8))),
        "norm_gains": jnp.clip(1.0 + 0.1 * jax.random.normal(streams_of[1], (2, D), jnp.float32), 0.5, 1.5).astype(jnp.bfloat16),
        "weights": noise(streams_of[2], (2, D, 4, INNER), D ** -0.5, 0.09375, ((0, 2), (1, 8), (3, 8))),
        "cotangent": noise(streams_of[3], (EXAMPLES, S, D), 1.0, 6.0, ((0, 8),)),
        "lengths": draw_lengths(jax.random.fold_in(streams_of[6], 71), 0),
        "dp_noise": noise(streams_of[5], (2, D, 4, INNER), 1.0, 6.0, ((0, 2), (1, 8), (3, 8)), jnp.float32),
    }


def rms_norm(values_in, gain_row):
    value32 = values_in.astype(jnp.float32)
    inverse = lax.rsqrt(lax.optimization_barrier(jnp.mean(value32 * value32, axis=-1, keepdims=True)) + 1e-06)
    return (value32 * inverse * gain_row.astype(jnp.float32)).astype(jnp.bfloat16)

def project(left, right):
    return jnp.dot(left, right, preferred_element_type=jnp.float32).astype(jnp.bfloat16)

def attend(queries, key_proj, value_proj, key_mask):
    seq_len = queries.shape[0]
    query_heads = queries.reshape(seq_len, -1, HEAD).astype(jnp.float32)
    key_heads = key_proj.reshape(seq_len, -1, HEAD).astype(jnp.float32)
    value_heads = value_proj.reshape(seq_len, -1, HEAD).astype(jnp.float32)
    scores = jnp.einsum('shd,thd->hst', query_heads, key_heads) * HEAD ** (-0.5)
    scores = jnp.where(key_mask[None, None, :], scores, -jnp.inf)
    attn_probs = jax.nn.softmax(scores, axis=-1)
    probs_low = attn_probs.astype(jnp.bfloat16).astype(jnp.float32)
    context = jnp.einsum('hst,thd->shd', probs_low, value_heads).reshape(seq_len, -1)
    return (attn_probs, context.astype(jnp.bfloat16))

def attend_back(queries, key_proj, value_proj, attn_probs, grad_ctx):
    seq_len = queries.shape[0]
    query_heads = queries.reshape(seq_len, -1, HEAD).astype(jnp.float32)
    key_heads = key_proj.reshape(seq_len, -1, HEAD).astype(jnp.float32)
    value_heads = value_proj.reshape(seq_len, -1, HEAD).astype(jnp.float32)
    grad_heads = grad_ctx.reshape(seq_len, -1, HEAD).astype(jnp.float32)
    grad_probs = jnp.einsum('shd,thd->hst', grad_heads, value_heads)
    inner_sum = lax.optimization_barrier(jnp.sum(grad_probs * attn_probs, axis=-1, keepdims=True))
    grad_scores = (attn_probs * (grad_probs - inner_sum) * HEAD ** (-0.5)).astype(jnp.bfloat16).astype(jnp.float32)
    probs_low = attn_probs.astype(jnp.bfloat16).astype(jnp.float32)
    grad_query = jnp.einsum('hst,thd->shd', grad_scores, key_heads).reshape(seq_len, -1)
    grad_key = jnp.einsum('hst,shd->thd', grad_scores, query_heads).reshape(seq_len, -1)
    grad_value = jnp.einsum('hst,shd->thd', probs_low, grad_heads).reshape(seq_len, -1)
    return (grad_query.astype(jnp.bfloat16), grad_key.astype(jnp.bfloat16), grad_value.astype(jnp.bfloat16))

def group_terms(left, right):
    seq_len = left.shape[0]
    left_groups = left.reshape(seq_len, N_MP, -1).astype(jnp.float32)
    right_groups = right.reshape(right.shape[0], N_MP, -1).astype(jnp.float32)
    return jnp.einsum('srj,drj->rsd', left_groups, right_groups)

def group_sum(terms):
    return lax.optimization_barrier(jnp.sum(terms.astype(jnp.bfloat16).astype(jnp.float32), axis=0))

def gram(matrix):
    return jnp.dot(matrix, matrix.T, preferred_element_type=jnp.float32)

def ghost(normed, kv_rows, grad_query, grad_key, grad_value, grad_out, context):
    first = jnp.sum(gram(normed) * gram(grad_query))
    second = jnp.sum(gram(kv_rows) * (gram(grad_key) + gram(grad_value)))
    third = jnp.sum(gram(grad_out) * gram(context))
    return first + second + third

def one_example(enc_in, dec_in, cot_rows, enc_len, dec_len, norm_gains, weights):
    positions = jnp.arange(S)
    key_mask = positions < enc_len
    enc_w = weights[0]
    dec_w = weights[1]
    normed_enc = rms_norm(enc_in, norm_gains[0])
    query_enc = project(normed_enc, enc_w[:, 0])
    key_enc = project(normed_enc, enc_w[:, 1])
    value_enc = project(normed_enc, enc_w[:, 2])
    probs_enc, context_enc = attend(query_enc, key_enc, value_enc, key_mask)
    enc_out = (enc_in.astype(jnp.float32) + group_sum(group_terms(context_enc, enc_w[:, 3]))).astype(jnp.bfloat16)
    normed_dec = rms_norm(dec_in, norm_gains[1])
    query_dec = project(normed_dec, dec_w[:, 0])
    key_dec = project(enc_out, dec_w[:, 1])
    value_dec = project(enc_out, dec_w[:, 2])
    probs_dec, context_dec = attend(query_dec, key_dec, value_dec, key_mask)
    grad_out_dec = cot_rows * (positions < dec_len).astype(jnp.bfloat16)[:, None]
    grad_ctx_dec = project(grad_out_dec, dec_w[:, 3])
    gq_dec, gk_dec, gv_dec = attend_back(query_dec, key_dec, value_dec, probs_dec, grad_ctx_dec)
    grad_enc = group_sum(group_terms(gk_dec, dec_w[:, 1]) + group_terms(gv_dec, dec_w[:, 2])).astype(jnp.bfloat16)
    grad_ctx_enc = project(grad_enc, enc_w[:, 3])
    gq_enc, gk_enc, gv_enc = attend_back(query_enc, key_enc, value_enc, probs_enc, grad_ctx_enc)
    sq_norm = ghost(normed_enc, normed_enc, gq_enc, gk_enc, gv_enc, grad_enc, context_enc)
    sq_norm = sq_norm + ghost(normed_dec, enc_out, gq_dec, gk_dec, gv_dec, grad_out_dec, context_dec)
    enc_pairs = (normed_enc, gq_enc, normed_enc, gk_enc, normed_enc, gv_enc, grad_enc, context_enc)
    dec_pairs = (normed_dec, gq_dec, enc_out, gk_dec, enc_out, gv_dec, grad_out_dec, context_dec)
    return (sq_norm, enc_pairs, dec_pairs)

def weighted_sum(left_all, right_all, clip_scale):
    left_groups = left_all.reshape(N_DP, MB, S, left_all.shape[-1])
    right_groups = right_all.reshape(N_DP, MB, S, right_all.shape[-1])
    scale_groups = clip_scale.reshape(N_DP, MB)

    def add_group(carry, items):
        left_block, right_block, scale_block = items
        partial_value = jnp.einsum('i,isd,isj->dj', scale_block, left_block.astype(jnp.float32), right_block.astype(jnp.float32))
        return (carry + partial_value.astype(jnp.bfloat16).astype(jnp.float32), None)
    start_sum = jnp.zeros((left_all.shape[-1], right_all.shape[-1]), jnp.float32)
    result, unused = lax.scan(add_group, start_sum, (left_groups, right_groups, scale_groups))
    return result

def reference(inputs, norm_gains, weights, cotangent, lengths, dp_noise):
    run = jax.vmap(one_example, in_axes=(0, 0, 0, 0, 0, None, None))
    sq_norm, enc_pairs, dec_pairs = run(inputs[0], inputs[1], cotangent, lengths[0], lengths[1], norm_gains, weights)
    bound = jnp.sqrt(jnp.float32(8.0 * D * INNER))
    clip_scale = bound / (jnp.sqrt(sq_norm) + 0.01 * bound)
    layers = []
    for pairs in (enc_pairs, dec_pairs):
        mats = [weighted_sum(pairs[2 * slot], pairs[2 * slot + 1], clip_scale) for slot in range(4)]
        layers.append(jnp.stack(mats, axis=1))
    summed = jnp.stack(layers, axis=0)
    noisy_grad = (summed + dp_noise) / EXAMPLES
    return (noisy_grad, clip_scale)
```

```python
import functools

import jax
import jax.numpy as jnp
from jax import lax
from jax.experimental import pallas as pl
from jax.experimental.pallas import tpu as pltpu
from jax.sharding import PartitionSpec as P

D = 4096
HEADS = 64
HEAD = 64
MESH = pl.DeviceIdType.MESH
F32 = jnp.float32
BF16 = jnp.bfloat16
N = 8
ROWS = 256
PIECE = 512
CHUNKS = 4
CH = ROWS // CHUNKS
ANY = pl.BlockSpec(memory_space=pl.ANY)
HBM = pl.BlockSpec(memory_space=pltpu.HBM)
VM = pl.BlockSpec(memory_space=pltpu.VMEM)
SM = pl.BlockSpec(memory_space=pltpu.SMEM)
DMA = pltpu.SemaphoreType.DMA


def rc(src, dst, send_sem, recv_sem, dev):
    return pltpu.make_async_remote_copy(
        src_ref=src,
        dst_ref=dst,
        send_sem=send_sem,
        recv_sem=recv_sem,
        device_id=dev,
        device_id_type=MESH,
    )


def coords():
    return lax.axis_index("section"), lax.axis_index("dp"), lax.axis_index("mp")


def greet(devs, extra=None):
    barrier = pltpu.get_barrier_semaphore()
    for dev in devs:
        pl.semaphore_signal(barrier, inc=1, device_id=dev, device_id_type=MESH)
    if extra is not None:
        cond, dev = extra

        @pl.when(cond)
        def _():
            pl.semaphore_signal(barrier, inc=1, device_id=dev, device_id_type=MESH)

        pl.semaphore_wait(barrier, len(devs) + jnp.where(cond, 1, 0))
    else:
        pl.semaphore_wait(barrier, len(devs))


def mp_peers(s, d, m):
    return [(s, d, (m + i) % N) for i in range(1, N)]


def dp_near(s, d, m):
    return [(s, (d + 2) % N, m), (s, (d + 6) % N, m), (s, d + 1 - 2 * (d % 2), m)]


class DpGather:
    def __init__(self, count, own, dst, half, send, recv, local):
        self.n, self.own, self.dst, self.half = count, own, dst, half
        self.send, self.recv, self.local = send, recv, local
        s, d, m = coords()
        self.d = d
        self.left, self.right, self.far = (d + 6) % N, (d + 2) % N, (d + 4) % N
        self.sib = d + 1 - 2 * (d % 2)
        self.to_right, self.to_left = (s, self.right, m), (s, self.left, m)
        self.to_sib = (s, self.sib, m)

    def cp(self, j, kind, src, dst, dev):
        return rc(src, dst, self.send.at[j, kind], self.recv.at[j, kind], dev)

    def keep(self, j):
        return pltpu.make_async_copy(self.own(j), self.dst(j, self.d), self.local.at[j])

    def out(self, j, kind):
        d = self.d
        if kind == 0:
            return self.cp(j, 0, self.own(j), self.dst(j, d), self.to_right)
        if kind == 1:
            return self.cp(j, 1, self.own(j), self.dst(j, d), self.to_left)
        if kind == 2:
            ref = self.half(j, self.left, 0)
            return self.cp(j, 2, ref, ref, self.to_right)
        if kind == 3:
            ref = self.half(j, self.right, 1)
            return self.cp(j, 3, ref, ref, self.to_left)
        if kind == 4:
            return self.cp(j, 4, self.own(j), self.dst(j, d), self.to_sib)
        block = (self.left, self.right, self.far)[kind - 5]
        return self.cp(j, kind, self.dst(j, block), self.dst(j, block), self.to_sib)

    def into(self, j, kind):
        sib = self.sib
        if kind == 0:
            ref = self.dst(j, self.left)
        elif kind == 1:
            ref = self.dst(j, self.right)
        elif kind == 2:
            ref = self.half(j, self.far, 0)
        elif kind == 3:
            ref = self.half(j, self.far, 1)
        else:
            ref = self.dst(j, (sib, (sib + 6) % N, (sib + 2) % N, (sib + 4) % N)[kind - 4])
        return self.cp(j, kind, ref, ref, self.to_sib)

    def begin(self, j):
        self.out(j, 0).start()
        self.out(j, 1).start()
        self.out(j, 4).start()
        self.keep(j).start()

    def open(self):
        for j in range(min(2, self.n)):
            self.begin(j)

    def far_on(self, j):
        self.into(j, 2).wait_recv()
        self.into(j, 3).wait_recv()
        self.out(j, 7).start()

    def middle(self, j):
        self.into(j, 0).wait_recv()
        self.into(j, 1).wait_recv()
        self.out(j, 2).start()
        self.out(j, 3).start()
        self.out(j, 5).start()
        self.out(j, 6).start()
        if j + 2 < self.n:
            self.begin(j + 2)
        if j > 0:
            self.far_on(j - 1)

    def close(self):
        self.far_on(self.n - 1)
        for j in range(self.n):
            for kind in range(4, 8):
                self.into(j, kind).wait_recv()
            for kind in range(8):
                self.out(j, kind).wait_send()
            self.keep(j).wait()


class SliceGather:
    def __init__(self, source, turn, dest, send_t, recv_t, local_t, send, recv, local):
        s, d, m = coords()
        self.s, self.d, self.m = s, d, m
        self.source, self.turn, self.dest = source, turn, dest
        self.send_t, self.recv_t, self.local_t = send_t, recv_t, local_t
        self.send, self.recv, self.local = send, recv, local
        self.far = rc(source, turn, send_t, recv_t, (s, m, d))
        self.near = pltpu.make_async_copy(source, turn, local_t)

    def open(self):
        pl.when(self.d != self.m)(lambda: self.far.start())
        pl.when(self.d == self.m)(lambda: self.near.start())

    def rows(self, m):
        return self.dest.at[pl.ds(pl.multiple_of(m * ROWS, ROWS), ROWS)]

    def hand(self, i):
        return rc(
            self.turn,
            self.rows(self.m),
            self.send.at[i - 1],
            self.recv.at[i - 1],
            (self.s, self.d, (self.m + i) % N),
        )

    def taken(self, i):
        ref = self.rows((self.m + N - i) % N)
        return rc(ref, ref, self.send.at[i - 1], self.recv.at[i - 1], (self.s, self.d, (self.m + i) % N))

    def keep(self):
        return pltpu.make_async_copy(self.turn, self.rows(self.m), self.local)

    def middle(self):
        pl.when(self.d != self.m)(lambda: self.far.wait_recv())
        pl.when(self.d == self.m)(lambda: self.near.wait())
        for i in range(1, N):
            self.hand(i).start()
        self.keep().start()

    def close(self):
        for i in range(1, N):
            self.taken(i).wait_recv()
        for i in range(1, N):
            self.hand(i).wait_send()
        self.keep().wait()
        pl.when(self.d != self.m)(lambda: self.far.wait_send())


def piece(ref, m, rows=None):
    cols = pl.ds(pl.multiple_of(m * PIECE, PIECE), PIECE)
    if rows is None:
        return ref.at[:, cols]
    return ref.at[pl.ds(rows, CH), cols]


def gather_kernel(wt, xa, xb, full, slices, turn, w_send, w_recv, w_loc, t_send, t_recv, t_loc, b_send, b_recv, b_loc):
    s, d, m = coords()
    greet(mp_peers(s, d, m) + dp_near(s, d, m), (d != m, (s, m, d)))
    gather = DpGather(
        4,
        lambda j: wt.at[j],
        lambda j, b: full.at[j, b],
        lambda j, b, h: full.at[j, b, pl.ds(h * 256, 256)],
        w_send,
        w_recv,
        w_loc,
    )
    slots = [
        SliceGather(
            piece(ref, m),
            turn.at[i],
            slices.at[i],
            t_send.at[i],
            t_recv.at[i],
            t_loc.at[i],
            b_send.at[i],
            b_recv.at[i],
            b_loc.at[i],
        )
        for i, ref in enumerate((xa, xb))
    ]
    gather.open()
    slots[0].open()
    pl.when(s == 1)(slots[1].open)
    gather.middle(0)
    slots[0].middle()
    pl.when(s == 1)(slots[1].middle)
    for j in range(1, 4):
        gather.middle(j)
    gather.close()
    slots[0].close()
    pl.when(s == 1)(slots[1].close)


def gather_weights(wt, xa, xb):
    return pl.pallas_call(
        gather_kernel,
        name="gather_weights",
        out_shape=(
            jax.ShapeDtypeStruct((4, N, PIECE, PIECE), BF16),
            jax.ShapeDtypeStruct((3, N * ROWS, PIECE), BF16),
        ),
        in_specs=[VM, ANY, ANY],
        out_specs=(HBM, HBM),
        scratch_shapes=[
            pltpu.VMEM((2, ROWS, PIECE), BF16),
            DMA((4, 8)),
            DMA((4, 8)),
            DMA((4,)),
            DMA((2,)),
            DMA((2,)),
            DMA((2,)),
            DMA((2, 7)),
            DMA((2, 7)),
            DMA((2,)),
        ],
        compiler_params=pltpu.CompilerParams(collective_id=0, has_side_effects=True),
    )(wt, xa, xb)


class Relay:
    def __init__(self, first, terms, resid, total, recv_buf, own, res, summed, landed, sems):
        self.first, self.terms, self.resid, self.total = first, terms, resid, total
        self.recv_buf, self.own, self.res, self.summed, self.landed = recv_buf, own, res, summed, landed
        self.s_send, self.s_recv, self.h_send, self.h_recv, self.g_send, self.g_recv, self.loc = sems
        self.s, self.d, self.m = coords()
        self.partner = (1 - self.s, self.d, self.m)

    def peer(self, i):
        return (self.s, self.d, (self.m + i) % N)

    def scatter(self, c, i):
        return rc(
            piece(self.terms, (self.m + i) % N, c * CH),
            self.recv_buf.at[i - 1, pl.ds(c * CH, CH)],
            self.s_send.at[c, i - 1],
            self.s_recv.at[c, i - 1],
            self.peer(i),
        )

    def hand(self, c):
        rows = pl.ds(c * CH, CH)
        return rc(self.summed.at[rows], self.landed.at[rows], self.h_send.at[c], self.h_recv.at[c], self.partner)

    def spread(self, c, i):
        return rc(
            self.landed.at[pl.ds(c * CH, CH)],
            piece(self.total, self.m, c * CH),
            self.g_send.at[c, i - 1],
            self.g_recv.at[c, i - 1],
            self.peer(i),
        )

    def taken(self, c, i):
        ref = piece(self.total, (self.m + N - i) % N, c * CH)
        return rc(ref, ref, self.g_send.at[c, i - 1], self.g_recv.at[c, i - 1], self.peer(i))

    def keep(self, c):
        return pltpu.make_async_copy(
            self.landed.at[pl.ds(c * CH, CH)], piece(self.total, self.m, c * CH), self.loc.at[c]
        )

    def sender_open(self):
        for c in range(CHUNKS):
            for i in range(1, N):
                self.scatter(c, i).start()
        own = pltpu.make_async_copy(piece(self.terms, self.m), self.own, self.loc.at[0])
        own.start()
        if self.resid is not None:
            res = pltpu.make_async_copy(piece(self.resid, self.m), self.res, self.loc.at[1])
            res.start()
            res.wait()
        own.wait()

    def sender_rest(self):
        for c in range(CHUNKS):
            rows = pl.ds(c * CH, CH)
            for i in range(1, N):
                self.scatter(c, i).wait_recv()
            acc = self.own[rows].astype(F32)
            for i in range(1, N):
                acc = acc + self.recv_buf[i - 1, rows].astype(F32)
            if self.resid is not None:
                acc = acc + self.res[rows].astype(F32)
            self.summed[rows] = acc.astype(BF16)
            self.hand(c).start()
        for c in range(CHUNKS):
            for i in range(1, N):
                self.scatter(c, i).wait_send()
            self.hand(c).wait_send()

    def taker(self):
        for c in range(CHUNKS):
            self.hand(c).wait_recv()
            for i in range(1, N):
                self.spread(c, i).start()
            self.keep(c).start()
        for c in range(CHUNKS):
            for i in range(1, N):
                self.taken(c, i).wait_recv()
            for i in range(1, N):
                self.spread(c, i).wait_send()
            self.keep(c).wait()


RELAY_SCRATCH = [
    pltpu.VMEM((7, ROWS, PIECE), BF16),
    pltpu.VMEM((ROWS, PIECE), BF16),
    pltpu.VMEM((ROWS, PIECE), BF16),
    pltpu.VMEM((ROWS, PIECE), BF16),
    pltpu.VMEM((ROWS, PIECE), BF16),
    DMA((CHUNKS, 7)),
    DMA((CHUNKS, 7)),
    DMA((CHUNKS,)),
    DMA((CHUNKS,)),
    DMA((CHUNKS, 7)),
    DMA((CHUNKS, 7)),
    DMA((CHUNKS,)),
]


def forward_kernel(terms, resid, total, recv_buf, own, res, summed, landed, *sems):
    s, d, m = coords()
    greet(mp_peers(s, d, m) + [(1 - s, d, m)])
    relay = Relay(0, terms, resid, total, recv_buf, own, res, summed, landed, sems)

    @pl.when(s == 0)
    def _():
        relay.sender_open()
        relay.sender_rest()

    pl.when(s == 1)(relay.taker)


def relay_forward(terms, resid):
    return pl.pallas_call(
        forward_kernel,
        name="relay_forward",
        out_shape=jax.ShapeDtypeStruct((ROWS, D), BF16),
        in_specs=[ANY, ANY],
        out_specs=HBM,
        scratch_shapes=list(RELAY_SCRATCH),
        compiler_params=pltpu.CompilerParams(collective_id=1, has_side_effects=True),
    )(terms, resid)


def backward_kernel(terms, ctx, before, total, rights, recv_buf, own, res, summed, landed, *sems):
    s, d, m = coords()
    greet(mp_peers(s, d, m) + dp_near(s, d, m) + [(1 - s, d, m)])
    relay_sems, (y_send, y_recv, y_loc) = sems[:7], sems[7:]
    relay = Relay(1, terms, None, total, recv_buf, own, res, summed, landed, relay_sems)
    gather = DpGather(
        1,
        lambda j: ctx,
        lambda j, b: rights.at[3, pl.ds(pl.multiple_of(b * ROWS, ROWS), ROWS)],
        lambda j, b, h: rights.at[3, pl.ds(pl.multiple_of(b * ROWS + h * 128, 128), 128)],
        y_send,
        y_recv,
        y_loc,
    )
    pl.when(s == 1)(relay.sender_open)
    gather.open()
    pl.when(s == 1)(relay.sender_rest)
    gather.middle(0)
    gather.close()
    pl.when(s == 0)(relay.taker)


def relay_backward(terms, ctx, before):
    return pl.pallas_call(
        backward_kernel,
        name="relay_backward",
        out_shape=(
            jax.ShapeDtypeStruct((ROWS, D), BF16),
            jax.ShapeDtypeStruct((4, N * ROWS, PIECE), BF16),
        ),
        in_specs=[ANY, VM, HBM],
        out_specs=(HBM, HBM),
        scratch_shapes=list(RELAY_SCRATCH) + [DMA((1, 8)), DMA((1, 8)), DMA((1,))],
        input_output_aliases={2: 0},
        compiler_params=pltpu.CompilerParams(collective_id=2, has_side_effects=True),
    )(terms, ctx, before)


def final_kernel(
    gq, gk, gv, relayed, norm, slices_in, rights_in, slices, rights, norms,
    turn, norm_mp, norm_own, norm_far, norm_dp,
    y_send, y_recv, y_loc, t_send, t_recv, t_loc, b_send, b_recv, b_loc, n_send, n_recv, f_send, f_recv, e_send, e_recv,
):
    s, d, m = coords()
    dp_all = [(s, (d + i) % N, m) for i in range(1, N)]
    greet(mp_peers(s, d, m) + dp_all + [(1 - s, d, m)], (d != m, (s, m, d)))
    parts = (gq, gk, gv)
    gather = DpGather(
        3,
        lambda j: parts[j],
        lambda j, b: rights.at[j, pl.ds(pl.multiple_of(b * ROWS, ROWS), ROWS)],
        lambda j, b, h: rights.at[j, pl.ds(pl.multiple_of(b * ROWS + h * 128, 128), 128)],
        y_send,
        y_recv,
        y_loc,
    )
    slot = SliceGather(
        piece(relayed, m), turn, slices.at[2], t_send, t_recv, t_loc, b_send, b_recv, b_loc
    )

    def to_mp(i):
        return rc(norm, norm_mp.at[m], n_send.at[i - 1], n_recv.at[i - 1], (s, d, (m + i) % N))

    def from_mp(i):
        ref = norm_mp.at[(m + N - i) % N]
        return rc(ref, ref, n_send.at[i - 1], n_recv.at[i - 1], (s, d, (m + i) % N))

    def to_dp(i):
        return rc(norm_dp, norms.at[d], e_send.at[i - 1], e_recv.at[i - 1], (s, (d + i) % N, m))

    def from_dp(i):
        ref = norms.at[(d + N - i) % N]
        return rc(ref, ref, e_send.at[i - 1], e_recv.at[i - 1], (s, (d + i) % N, m))

    for i in range(1, N):
        to_mp(i).start()
    slot.open()
    gather.open()
    norm_mp[m] = norm[...]
    for i in range(1, N):
        from_mp(i).wait_recv()
    acc = norm_mp[0]
    for i in range(1, N):
        acc = acc + norm_mp[i]
    norm_own[...] = acc
    over = rc(norm_own, norm_far, f_send, f_recv, (1 - s, d, m))
    over.start()
    slot.middle()
    gather.middle(0)
    over.wait_recv()
    both = norm_own[...] + norm_far[...]
    norm_dp[...] = both
    norms[d] = both
    for i in range(1, N):
        to_dp(i).start()
    gather.middle(1)
    gather.middle(2)
    gather.close()
    slot.close()
    for i in range(1, N):
        from_dp(i).wait_recv()
    for i in range(1, N):
        to_mp(i).wait_send()
        to_dp(i).wait_send()
    over.wait_send()


def gather_grads(gq, gk, gv, relayed, norm, slices, rights):
    small = pltpu.VMEM((8, 128), F32)
    return pl.pallas_call(
        final_kernel,
        name="gather_grads",
        out_shape=(
            jax.ShapeDtypeStruct(slices.shape, BF16),
            jax.ShapeDtypeStruct(rights.shape, BF16),
            jax.ShapeDtypeStruct((N, 8, 128), F32),
        ),
        in_specs=[VM, VM, VM, ANY, VM, HBM, HBM],
        out_specs=(HBM, HBM, VM),
        scratch_shapes=[
            pltpu.VMEM((ROWS, PIECE), BF16),
            pltpu.VMEM((N, 8, 128), F32),
            small,
            small,
            small,
            DMA((3, 8)),
            DMA((3, 8)),
            DMA((3,)),
            DMA,
            DMA,
            DMA,
            DMA((7,)),
            DMA((7,)),
            DMA,
            DMA((7,)),
            DMA((7,)),
            DMA,
            DMA,
            DMA((7,)),
            DMA((7,)),
        ],
        input_output_aliases={5: 0, 6: 1},
        compiler_params=pltpu.CompilerParams(collective_id=3, has_side_effects=True),
    )(gq, gk, gv, relayed, norm, slices, rights)


def dot_nt(a, b):
    return lax.dot_general(a, b, (((1,), (1,)), ((), ())), preferred_element_type=F32)


def dot_nn(a, b):
    return lax.dot_general(a, b, (((1,), (0,)), ((), ())), preferred_element_type=F32)


def dot_tn(a, b):
    return lax.dot_general(a, b, (((0,), (0,)), ((), ())), preferred_element_type=F32)


def head_masks():
    lane = lax.broadcasted_iota(jnp.int32, (128, 128), 1)
    return lane < HEAD, lane >= HEAD


def soft(q, k, mask, key_ok):
    zero = jnp.zeros_like(q)
    scores = dot_nt(jnp.where(mask, q, zero), k) * HEAD ** (-0.5)
    scores = jnp.where(key_ok, scores, -jnp.inf)
    weights = jnp.exp(scores - jnp.max(scores, axis=-1, keepdims=True))
    return weights / jnp.sum(weights, axis=-1, keepdims=True)


def attend_kernel(lens, q_ref, k_ref, v_ref, ctx_ref):
    key_ok = lax.broadcasted_iota(jnp.int32, (128, 128), 1) < lens[pl.program_id(0)]
    masks = head_masks()
    for pair in range(4):
        cols = slice(pair * 128, pair * 128 + 128)
        q, k, v = q_ref[:, cols], k_ref[:, cols], v_ref[:, cols]
        zero = jnp.zeros_like(q)
        ctx = jnp.zeros((128, 128), F32)
        for mask in masks:
            probs = soft(q, k, mask, key_ok)
            ctx = ctx + dot_nn(probs.astype(BF16), jnp.where(mask, v, zero))
        ctx_ref[:, cols] = ctx.astype(BF16)


def attend(lens, q, k, v):
    spec = pl.BlockSpec((128, PIECE), lambda e: (e, 0))
    return pl.pallas_call(
        attend_kernel,
        name="attend",
        grid=(2,),
        in_specs=[SM] + [spec] * 3,
        out_specs=spec,
        out_shape=jax.ShapeDtypeStruct((ROWS, PIECE), BF16),
    )(lens, q, k, v)


def attend_all_kernel(lens, q_ref, k_ref, v_ref, g_ref, ctx_ref, gq_ref, gk_ref, gv_ref):
    key_ok = lax.broadcasted_iota(jnp.int32, (128, 128), 1) < lens[pl.program_id(0)]
    masks = head_masks()
    for pair in range(4):
        cols = slice(pair * 128, pair * 128 + 128)
        q, k, v, g = q_ref[:, cols], k_ref[:, cols], v_ref[:, cols], g_ref[:, cols]
        zero = jnp.zeros_like(q)
        ctx = gq = gk = gv = jnp.zeros((128, 128), F32)
        for mask in masks:
            probs = soft(q, k, mask, key_ok)
            low = probs.astype(BF16)
            g_one = jnp.where(mask, g, zero)
            gp = dot_nt(g_one, v)
            inner = jnp.sum(gp * probs, axis=-1, keepdims=True)
            gs = (probs * (gp - inner) * HEAD ** (-0.5)).astype(BF16)
            ctx = ctx + dot_nn(low, jnp.where(mask, v, zero))
            gq = gq + dot_nn(gs, jnp.where(mask, k, zero))
            gk = gk + dot_tn(gs, jnp.where(mask, q, zero))
            gv = gv + dot_tn(low, g_one)
        ctx_ref[:, cols] = ctx.astype(BF16)
        gq_ref[:, cols] = gq.astype(BF16)
        gk_ref[:, cols] = gk.astype(BF16)
        gv_ref[:, cols] = gv.astype(BF16)


def attend_all(lens, q, k, v, g):
    spec = pl.BlockSpec((128, PIECE), lambda e: (e, 0))
    shape = jax.ShapeDtypeStruct((ROWS, PIECE), BF16)
    return pl.pallas_call(
        attend_all_kernel,
        name="attend_all",
        grid=(2,),
        in_specs=[SM] + [spec] * 4,
        out_specs=(spec,) * 4,
        out_shape=(shape,) * 4,
    )(lens, q, k, v, g)


def norm_kernel(sec, xa, xb, xr, gq, gk, gv, ctx, out):
    example = pl.program_id(0)
    is_dec = sec[0] == 1

    def gram(ref):
        return dot_nt(ref[...], ref[...])

    kv, cc = gram(gk) + gram(gv), gram(ctx)
    none = jnp.zeros_like(cc)
    total = gram(xa) * (gram(gq) + jnp.where(is_dec, none, kv))
    total = total + gram(xr) * jnp.where(is_dec, kv, cc) + gram(xb) * jnp.where(is_dec, cc, none)
    value = jnp.sum(total)
    lane = lax.broadcasted_iota(jnp.int32, (8, 128), 1)
    mine = jnp.where(lane == example, value, 0.0)

    @pl.when(example == 0)
    def _():
        out[...] = mine

    @pl.when(example == 1)
    def _():
        out[...] += mine


def norm_parts(sec, xa, xb, xr, gq, gk, gv, ctx):
    wide = pl.BlockSpec((128, D), lambda e: (e, 0))
    thin = pl.BlockSpec((128, PIECE), lambda e: (e, 0))
    return pl.pallas_call(
        norm_kernel,
        name="norm_parts",
        grid=(2,),
        in_specs=[SM] + [wide] * 3 + [thin] * 4,
        out_specs=pl.BlockSpec((8, 128), lambda e: (0, 0)),
        out_shape=jax.ShapeDtypeStruct((8, 128), F32),
    )(sec, xa, xb, xr, gq, gk, gv, ctx)


BLOCK = 128


def weight_kernel(sec, clip, x_ref, y_ref, noise_ref, out_ref, scaled):
    @pl.when(pl.program_id(0) == 0)
    def _():
        for mat in range(4):

            @pl.loop(0, 16)
            def _(e):
                rows = pl.ds(pl.multiple_of(e * 128, 128), 128)
                scaled[mat, rows] = (y_ref[mat, rows].astype(F32) * clip[e]).astype(BF16)

    is_dec = sec[0]
    picks = (0, 2 * is_dec, 2 * is_dec, 2 - is_dec)
    for mat in range(4):
        total = dot_tn(x_ref[picks[mat]], scaled[mat])
        out_ref[:, mat, :] = (total + noise_ref[:, mat, :]) * (1.0 / 16.0)


def weight_grads(sec, clip, slices, rights, dp_noise):
    wide = pl.BlockSpec((BLOCK, 4, PIECE), lambda b: (b, 0, 0))
    return pl.pallas_call(
        weight_kernel,
        name="weight_grads",
        grid=(PIECE // BLOCK,),
        in_specs=[
            SM,
            SM,
            pl.BlockSpec((3, N * ROWS, BLOCK), lambda b: (0, 0, b)),
            pl.BlockSpec((4, N * ROWS, PIECE), lambda b: (0, 0, 0), pipeline_mode=pl.Buffered(1)),
            wide,
        ],
        out_specs=wide,
        out_shape=jax.ShapeDtypeStruct((PIECE, 4, PIECE), F32),
        scratch_shapes=[pltpu.VMEM((4, N * ROWS, PIECE), BF16)],
    )(sec, clip, slices, rights, dp_noise)


def rms_norm(values_in, gain_row):
    value32 = values_in.astype(F32)
    inverse = lax.rsqrt(jnp.mean(value32 * value32, axis=-1, keepdims=True) + 1e-06)
    return (value32 * inverse * gain_row.astype(F32)).astype(BF16)


def project(left, right):
    return jnp.dot(left, right, preferred_element_type=F32).astype(BF16)


def back_term(left, right):
    return jnp.einsum("sj,dj->sd", left, right, preferred_element_type=F32)


def per_device(inputs, norm_gains, weights, cotangent, lengths, dp_noise):
    section = lax.axis_index("section")
    is_dec = section == 1
    sec = jnp.reshape(section, (1,)).astype(jnp.int32)
    own_inputs = inputs[0].reshape(ROWS, D)
    normed = rms_norm(own_inputs, norm_gains[0])
    positions = jnp.arange(128)
    keep = (positions[None, :] < lengths[1][:, None]).astype(BF16)
    gout = (cotangent * keep[:, :, None]).reshape(ROWS, D)
    wt = jnp.swapaxes(weights[0], 0, 1)
    full, slices = gather_weights(wt, normed, gout)
    mats = full.reshape(4, D, PIECE)
    lens = lengths[0]
    thin = jnp.zeros((ROWS, PIECE), BF16)
    wide = jnp.zeros((ROWS, D), BF16)

    def first_dec():
        return project(normed, mats[0]), thin, thin, project(gout, mats[3]), thin, wide

    def first_enc():
        q, k, v = (project(normed, mats[i]) for i in range(3))
        ctx = attend(lens, q, k, v)
        return q, k, v, thin, ctx, back_term(ctx, mats[3]).astype(BF16)

    q, k, v, gctx, ctx, terms = lax.cond(is_dec, first_dec, first_enc)
    relayed = relay_forward(terms, own_inputs)

    def second_dec():
        k, v = project(relayed, mats[1]), project(relayed, mats[2])
        ctx, gq, gk, gv = attend_all(lens, q, k, v, gctx)
        terms = (back_term(gk, mats[1]) + back_term(gv, mats[2])).astype(BF16)
        return ctx, gq, gk, gv, terms

    def second_enc():
        return ctx, thin, thin, thin, wide

    ctx, gq, gk, gv, terms = lax.cond(is_dec, second_dec, second_enc)
    relayed, rights = relay_backward(terms, ctx, relayed)

    def third_dec():
        return gq, gk, gv

    def third_enc():
        _, gq, gk, gv = attend_all(lens, q, k, v, project(relayed, mats[3]))
        return gq, gk, gv

    gq, gk, gv = lax.cond(is_dec, third_dec, third_enc)
    norm = norm_parts(sec, normed, gout, relayed, gq, gk, gv, ctx)
    slices, rights, norms = gather_grads(gq, gk, gv, relayed, norm, slices, rights)
    sq_norm = norms[:, 0, :2]
    bound = jnp.sqrt(jnp.float32(8.0 * D * HEADS * HEAD))
    clip_all = bound / (jnp.sqrt(sq_norm) + 0.01 * bound)
    clip_scale = lax.dynamic_index_in_dim(clip_all, lax.axis_index("dp"), 0, keepdims=False)
    noisy_grad = weight_grads(sec, clip_all.reshape(16), slices, rights, dp_noise[0])
    return (noisy_grad[None], clip_scale)


def solution(mesh):
    placed = (
        P("section", "dp", None, None),
        P("section", None),
        P("section", "dp", None, "mp"),
        P("dp", None, None),
        P(None, "dp"),
        P("section", "dp", None, "mp"),
    )
    return jax.shard_map(
        per_device,
        mesh=mesh,
        in_specs=placed,
        out_specs=(P("section", "dp", None, "mp"), P("dp")),
        check_vma=False,
    )
```

```python
import functools

import jax
import jax.numpy as jnp
from jax import lax
from jax.experimental import pallas as pl
from jax.experimental.pallas import tpu as pltpu
from jax.sharding import PartitionSpec as P

D = 4096
HEADS = 64
HEAD = 64
MESH = pl.DeviceIdType.MESH
F32 = jnp.float32
BF16 = jnp.bfloat16
N = 8
ROWS = 256
PIECE = 512
CHUNKS = 4
CH = ROWS // CHUNKS
ANY = pl.BlockSpec(memory_space=pl.ANY)
HBM = pl.BlockSpec(memory_space=pltpu.HBM)
VM = pl.BlockSpec(memory_space=pltpu.VMEM)
SM = pl.BlockSpec(memory_space=pltpu.SMEM)
DMA = pltpu.SemaphoreType.DMA


def rc(src, dst, send_sem, recv_sem, dev):
    return pltpu.make_async_remote_copy(
        src_ref=src,
        dst_ref=dst,
        send_sem=send_sem,
        recv_sem=recv_sem,
        device_id=dev,
        device_id_type=MESH,
    )


def coords():
    return lax.axis_index("section"), lax.axis_index("dp"), lax.axis_index("mp")


def greet(devs, extra=None):
    barrier = pltpu.get_barrier_semaphore()
    for dev in devs:
        pl.semaphore_signal(barrier, inc=1, device_id=dev, device_id_type=MESH)
    if extra is not None:
        cond, dev = extra

        @pl.when(cond)
        def _():
            pl.semaphore_signal(barrier, inc=1, device_id=dev, device_id_type=MESH)

        pl.semaphore_wait(barrier, len(devs) + jnp.where(cond, 1, 0))
    else:
        pl.semaphore_wait(barrier, len(devs))


def mp_peers(s, d, m):
    return [(s, d, (m + i) % N) for i in range(1, N)]


def dp_near(s, d, m):
    return [(s, (d + 2) % N, m), (s, (d + 6) % N, m), (s, d + 1 - 2 * (d % 2), m)]


class DpGather:
    def __init__(self, count, own, dst, half, send, recv, local):
        self.n, self.own, self.dst, self.half = count, own, dst, half
        self.send, self.recv, self.local = send, recv, local
        s, d, m = coords()
        self.d = d
        self.left, self.right, self.far = (d + 6) % N, (d + 2) % N, (d + 4) % N
        self.sib = d + 1 - 2 * (d % 2)
        self.to_right, self.to_left = (s, self.right, m), (s, self.left, m)
        self.to_sib = (s, self.sib, m)

    def cp(self, j, kind, src, dst, dev):
        return rc(src, dst, self.send.at[j, kind], self.recv.at[j, kind], dev)

    def keep(self, j):
        return pltpu.make_async_copy(self.own(j), self.dst(j, self.d), self.local.at[j])

    def out(self, j, kind):
        d = self.d
        if kind == 0:
            return self.cp(j, 0, self.own(j), self.dst(j, d), self.to_right)
        if kind == 1:
            return self.cp(j, 1, self.own(j), self.dst(j, d), self.to_left)
        if kind == 2:
            ref = self.half(j, self.left, 0)
            return self.cp(j, 2, ref, ref, self.to_right)
        if kind == 3:
            ref = self.half(j, self.right, 1)
            return self.cp(j, 3, ref, ref, self.to_left)
        if kind == 4:
            return self.cp(j, 4, self.own(j), self.dst(j, d), self.to_sib)
        block = (self.left, self.right, self.far)[kind - 5]
        return self.cp(j, kind, self.dst(j, block), self.dst(j, block), self.to_sib)

    def into(self, j, kind):
        sib = self.sib
        if kind == 0:
            ref = self.dst(j, self.left)
        elif kind == 1:
            ref = self.dst(j, self.right)
        elif kind == 2:
            ref = self.half(j, self.far, 0)
        elif kind == 3:
            ref = self.half(j, self.far, 1)
        else:
            ref = self.dst(j, (sib, (sib + 6) % N, (sib + 2) % N, (sib + 4) % N)[kind - 4])
        return self.cp(j, kind, ref, ref, self.to_sib)

    def begin(self, j):
        self.out(j, 0).start()
        self.out(j, 1).start()
        self.out(j, 4).start()
        self.keep(j).start()

    def open(self):
        for j in range(min(2, self.n)):
            self.begin(j)

    def far_on(self, j):
        self.into(j, 2).wait_recv()
        self.into(j, 3).wait_recv()
        self.out(j, 7).start()

    def middle(self, j):
        self.into(j, 0).wait_recv()
        self.into(j, 1).wait_recv()
        self.out(j, 2).start()
        self.out(j, 3).start()
        self.out(j, 5).start()
        self.out(j, 6).start()
        if j + 2 < self.n:
            self.begin(j + 2)
        if j > 0:
            self.far_on(j - 1)

    def close(self):
        self.far_on(self.n - 1)
        for j in range(self.n):
            for kind in range(4, 8):
                self.into(j, kind).wait_recv()
            for kind in range(8):
                self.out(j, kind).wait_send()
            self.keep(j).wait()


class MpGather:
    def __init__(self, chunks, source, slot, send, recv, local):
        s, d, m = coords()
        self.chunks, self.source, self.slot = chunks, source, slot
        self.send, self.recv, self.local = send, recv, local
        x, y = m // 4, m % 4
        up, down, far = (y + 1) % 4, (y + 3) % 4, (y + 2) % 4
        self.m, self.xm = m, (1 - x) * 4 + y
        self.to = ((s, d, self.xm), (s, d, x * 4 + up), (s, d, x * 4 + down))
        self.sources = (m, m, m, self.xm, self.xm, down, 4 + up)
        self.landing = (
            self.xm,
            x * 4 + down,
            x * 4 + up,
            (1 - x) * 4 + down,
            (1 - x) * 4 + up,
            far,
            4 + far,
        )

    def out(self, c, kind):
        dest = self.slot(self.sources[kind], c)
        src = self.source(c) if kind < 3 else dest
        to = self.to[(0, 1, 2, 1, 2, 1, 2)[kind]]
        return rc(src, dest, self.send.at[c, kind], self.recv.at[c, kind], to)

    def into(self, c, kind):
        ref = self.slot(self.landing[kind], c)
        return rc(ref, ref, self.send.at[c, kind], self.recv.at[c, kind], self.to[0])

    def keep(self, c):
        return pltpu.make_async_copy(self.source(c), self.slot(self.m, c), self.local.at[c])

    def stage(self, c, number):
        if not 0 <= c < self.chunks:
            return
        waits, starts = (((), (0, 1, 2)), ((0,), (3, 4)), ((1, 2, 3, 4), (5, 6)), ((5, 6), ()))[number]
        for kind in waits:
            self.into(c, kind).wait_recv()
        for kind in starts:
            self.out(c, kind).start()
        if number == 0:
            self.keep(c).start()

    def close(self):
        for c in range(self.chunks):
            for kind in range(7):
                self.out(c, kind).wait_send()
            self.keep(c).wait()


def mp_near(s, d, m):
    x, y = m // 4, m % 4
    return [(s, d, (1 - x) * 4 + y), (s, d, x * 4 + (y + 1) % 4), (s, d, x * 4 + (y + 3) % 4)]


SLICE_CHUNKS = 2


class SliceGather:
    def __init__(self, source, turn, dest, send_t, recv_t, local_t, send, recv, local):
        s, d, m = coords()
        self.d, self.m = d, m
        self.far = lambda: rc(source, turn, send_t, recv_t, (s, m, d))
        self.near = lambda: pltpu.make_async_copy(source, turn, local_t)
        step = ROWS // SLICE_CHUNKS
        self.gather = MpGather(
            SLICE_CHUNKS,
            lambda c: turn.at[pl.ds(c * step, step)],
            lambda mm, c: dest.at[pl.ds(pl.multiple_of(mm * ROWS + c * step, step), step)],
            send,
            recv,
            local,
        )

    def open(self):
        pl.when(self.d != self.m)(lambda: self.far().start())
        pl.when(self.d == self.m)(lambda: self.near().start())

    def middle(self):
        pl.when(self.d != self.m)(lambda: self.far().wait_recv())
        pl.when(self.d == self.m)(lambda: self.near().wait())
        for c in range(SLICE_CHUNKS):
            self.gather.stage(c, 0)

    def second(self):
        for c in range(SLICE_CHUNKS):
            self.gather.stage(c, 1)

    def third(self):
        for c in range(SLICE_CHUNKS):
            self.gather.stage(c, 2)

    def close(self):
        for c in range(SLICE_CHUNKS):
            self.gather.stage(c, 3)
        self.gather.close()
        pl.when(self.d != self.m)(lambda: self.far().wait_send())


def piece(ref, m, rows=None):
    cols = pl.ds(pl.multiple_of(m * PIECE, PIECE), PIECE)
    if rows is None:
        return ref.at[:, cols]
    return ref.at[pl.ds(rows, CH), cols]


def gather_kernel(wt, xa, xb, full, slices, turn, w_send, w_recv, w_loc, t_send, t_recv, t_loc, b_send, b_recv, b_loc):
    s, d, m = coords()
    greet(mp_near(s, d, m) + dp_near(s, d, m), (d != m, (s, m, d)))
    gather = DpGather(
        4,
        lambda j: wt.at[j],
        lambda j, b: full.at[j, b],
        lambda j, b, h: full.at[j, b, pl.ds(h * 256, 256)],
        w_send,
        w_recv,
        w_loc,
    )
    slots = [
        SliceGather(
            piece(ref, m),
            turn.at[i],
            slices.at[i],
            t_send.at[i],
            t_recv.at[i],
            t_loc.at[i],
            b_send.at[i],
            b_recv.at[i],
            b_loc.at[i],
        )
        for i, ref in enumerate((xa, xb))
    ]
    gather.open()
    slots[0].open()
    pl.when(s == 1)(slots[1].open)
    slots[0].middle()
    pl.when(s == 1)(slots[1].middle)
    gather.middle(0)
    slots[0].second()
    pl.when(s == 1)(slots[1].second)
    gather.middle(1)
    slots[0].third()
    pl.when(s == 1)(slots[1].third)
    for j in range(2, 4):
        gather.middle(j)
    gather.close()
    slots[0].close()
    pl.when(s == 1)(slots[1].close)


def gather_weights(wt, xa, xb):
    return pl.pallas_call(
        gather_kernel,
        name="gather_weights",
        out_shape=(
            jax.ShapeDtypeStruct((4, N, PIECE, PIECE), BF16),
            jax.ShapeDtypeStruct((3, N * ROWS, PIECE), BF16),
        ),
        in_specs=[VM, ANY, ANY],
        out_specs=(HBM, HBM),
        scratch_shapes=[
            pltpu.VMEM((2, ROWS, PIECE), BF16),
            DMA((4, 8)),
            DMA((4, 8)),
            DMA((4,)),
            DMA((2,)),
            DMA((2,)),
            DMA((2,)),
            DMA((2, SLICE_CHUNKS, 7)),
            DMA((2, SLICE_CHUNKS, 7)),
            DMA((2, SLICE_CHUNKS)),
        ],
        compiler_params=pltpu.CompilerParams(collective_id=0, has_side_effects=True),
    )(wt, xa, xb)


class Relay:
    def __init__(self, terms, resid, total, bufs, sems):
        self.terms, self.resid = terms, resid
        (self.one, self.direct, self.passed, self.mixed, self.kept, self.cross, self.over, self.summed, self.landed) = bufs
        self.send, self.recv, g_send, g_recv, g_loc = sems
        s, d, m = coords()
        x, y = m // 4, m % 4
        self.x, self.y, self.m = x, y, m
        self.up, self.down, self.opp = (y + 1) % 4, (y + 3) % 4, (y + 2) % 4
        self.to_up, self.to_down = (s, d, x * 4 + self.up), (s, d, x * 4 + self.down)
        self.to_x = (s, d, (1 - x) * 4 + y)
        self.partner = (1 - s, d, (1 - x) * 4 + y)
        self.gather = MpGather(
            CHUNKS,
            lambda c: self.landed.at[self.rows(c)],
            lambda mm, c: piece(total, (mm + 4) % N, c * CH),
            g_send,
            g_recv,
            g_loc,
        )

    def rows(self, c):
        return pl.ds(c * CH, CH)

    def cp(self, c, kind, src, dst, to):
        return rc(src, dst, self.send.at[c, kind], self.recv.at[c, kind], to)

    def copy(self, c, kind):
        rows = self.rows(c)
        return (
            lambda: self.cp(c, 0, piece(self.terms, self.opp, c * CH), self.one.at[0, rows], self.to_up),
            lambda: self.cp(c, 1, piece(self.terms, 4 + self.opp, c * CH), self.one.at[1, rows], self.to_down),
            lambda: self.cp(c, 2, piece(self.terms, 4 + self.up, c * CH), self.direct.at[1, rows], self.to_up),
            lambda: self.cp(c, 3, piece(self.terms, self.down, c * CH), self.direct.at[0, rows], self.to_down),
            lambda: self.cp(c, 4, self.mixed.at[0, rows], self.passed.at[0, rows], self.to_up),
            lambda: self.cp(c, 5, self.mixed.at[1, rows], self.passed.at[1, rows], self.to_down),
            lambda: self.cp(c, 6, self.cross.at[rows], self.over.at[rows], self.to_x),
            lambda: self.cp(c, 7, self.summed.at[rows], self.landed.at[rows], self.partner),
        )[kind]()

    def mine(self, index, c):
        return self.terms[pl.ds(c * CH, CH), pl.ds(pl.multiple_of(index * PIECE, PIECE), PIECE)].astype(F32)

    def stage(self, c, number):
        if not 0 <= c < CHUNKS:
            return
        rows = self.rows(c)
        if number == 0:
            for kind in range(4):
                self.copy(c, kind).start()
        elif number == 1:
            for side, index in ((0, self.up), (1, 4 + self.down)):
                self.copy(c, side).wait_recv()
                value = self.one[side, rows].astype(F32) + self.mine(index, c)
                self.mixed[side, rows] = value.astype(BF16)
                self.copy(c, 4 + side).start()
        elif number == 2:
            for kind in range(2, 6):
                self.copy(c, kind).wait_recv()
            for side in range(2):
                value = self.direct[side, rows].astype(F32) + self.passed[side, rows].astype(F32)
                value = value + self.mine(side * 4 + self.y, c)

                @pl.when(self.x == side)
                def _():
                    self.kept[rows] = value

                @pl.when(self.x != side)
                def _():
                    self.cross[rows] = value.astype(BF16)

            self.copy(c, 6).start()
        else:
            self.copy(c, 6).wait_recv()
            value = self.kept[rows] + self.over[rows].astype(F32)
            if self.resid is not None:
                value = value + self.resid[rows].astype(F32)
            self.summed[rows] = value.astype(BF16)
            self.copy(c, 7).start()

    def sender(self):
        for tick in range(CHUNKS + 3):
            for number in range(4):
                self.stage(tick - number, number)
        for c in range(CHUNKS):
            for kind in range(8):
                self.copy(c, kind).wait_send()

    def taker(self):
        for tick in range(CHUNKS + 3):
            if tick < CHUNKS:
                self.copy(tick, 7).wait_recv()
            for number in range(4):
                self.gather.stage(tick - number, number)
        self.gather.close()


SIDES = pltpu.VMEM((2, ROWS, PIECE), BF16)
ONE = pltpu.VMEM((ROWS, PIECE), BF16)
RELAY_BUFS = [SIDES, SIDES, SIDES, SIDES, pltpu.VMEM((ROWS, PIECE), F32), ONE, ONE, ONE, ONE]
RELAY_SEMS = [DMA((CHUNKS, 8)), DMA((CHUNKS, 8)), DMA((CHUNKS, 7)), DMA((CHUNKS, 7)), DMA((CHUNKS,))]


def forward_kernel(terms, resid, total, *rest):
    s, d, m = coords()
    greet(mp_near(s, d, m) + [(1 - s, d, (m + 4) % N)])
    relay = Relay(terms, resid, total, rest[:9], rest[9:])
    pl.when(s == 0)(relay.sender)
    pl.when(s == 1)(relay.taker)


def relay_forward(terms, resid):
    return pl.pallas_call(
        forward_kernel,
        name="relay_forward",
        out_shape=jax.ShapeDtypeStruct((ROWS, D), BF16),
        in_specs=[VM, VM],
        out_specs=VM,
        scratch_shapes=RELAY_BUFS + RELAY_SEMS,
        compiler_params=pltpu.CompilerParams(collective_id=1, has_side_effects=True),
    )(terms, resid)


def backward_kernel(terms, ctx, before, total, rights, *rest):
    s, d, m = coords()
    greet(mp_near(s, d, m) + dp_near(s, d, m) + [(1 - s, d, (m + 4) % N)])
    relay = Relay(terms, None, total, rest[:9], rest[9:14])
    y_send, y_recv, y_loc, over = rest[14:]
    keep = pltpu.make_async_copy(before, total, over)
    gather = DpGather(
        1,
        lambda j: ctx,
        lambda j, b: rights.at[3, pl.ds(pl.multiple_of(b * ROWS, ROWS), ROWS)],
        lambda j, b, h: rights.at[3, pl.ds(pl.multiple_of(b * ROWS + h * 128, 128), 128)],
        y_send,
        y_recv,
        y_loc,
    )
    gather.open()

    @pl.when(s == 1)
    def _():
        keep.start()
        relay.sender()
        keep.wait()

    gather.middle(0)
    gather.close()
    pl.when(s == 0)(relay.taker)


def relay_backward(terms, ctx, before):
    return pl.pallas_call(
        backward_kernel,
        name="relay_backward",
        out_shape=(
            jax.ShapeDtypeStruct((ROWS, D), BF16),
            jax.ShapeDtypeStruct((4, N * ROWS, PIECE), BF16),
        ),
        in_specs=[VM, VM, VM],
        out_specs=(VM, HBM),
        scratch_shapes=RELAY_BUFS + RELAY_SEMS + [DMA((1, 8)), DMA((1, 8)), DMA((1,)), DMA],
        compiler_params=pltpu.CompilerParams(collective_id=2, has_side_effects=True),
    )(terms, ctx, before)


def final_kernel(
    gq, gk, gv, relayed, norm, slices_in, rights_in, slices, rights, norms,
    turn, norm_mp, norm_own, norm_far, norm_dp,
    y_send, y_recv, y_loc, t_send, t_recv, t_loc, b_send, b_recv, b_loc, n_send, n_recv, f_send, f_recv, e_send, e_recv,
):
    s, d, m = coords()
    dp_all = [(s, (d + i) % N, m) for i in range(1, N)]
    greet(mp_peers(s, d, m) + dp_all + [(1 - s, d, m)], (d != m, (s, m, d)))
    parts = (gq, gk, gv)
    gather = DpGather(
        3,
        lambda j: parts[j],
        lambda j, b: rights.at[j, pl.ds(pl.multiple_of(b * ROWS, ROWS), ROWS)],
        lambda j, b, h: rights.at[j, pl.ds(pl.multiple_of(b * ROWS + h * 128, 128), 128)],
        y_send,
        y_recv,
        y_loc,
    )
    slot = SliceGather(
        piece(relayed, m), turn, slices.at[2], t_send, t_recv, t_loc, b_send, b_recv, b_loc
    )

    def to_mp(i):
        return rc(norm, norm_mp.at[m], n_send.at[i - 1], n_recv.at[i - 1], (s, d, (m + i) % N))

    def from_mp(i):
        ref = norm_mp.at[(m + N - i) % N]
        return rc(ref, ref, n_send.at[i - 1], n_recv.at[i - 1], (s, d, (m + i) % N))

    def to_dp(i):
        return rc(norm_dp, norms.at[d], e_send.at[i - 1], e_recv.at[i - 1], (s, (d + i) % N, m))

    def from_dp(i):
        ref = norms.at[(d + N - i) % N]
        return rc(ref, ref, e_send.at[i - 1], e_recv.at[i - 1], (s, (d + i) % N, m))

    for i in range(1, N):
        to_mp(i).start()
    slot.open()
    gather.open()
    norm_mp[m] = norm[...]
    for i in range(1, N):
        from_mp(i).wait_recv()
    acc = norm_mp[0]
    for i in range(1, N):
        acc = acc + norm_mp[i]
    norm_own[...] = acc
    over = rc(norm_own, norm_far, f_send, f_recv, (1 - s, d, m))
    over.start()
    gather.middle(0)
    slot.middle()
    over.wait_recv()
    both = norm_own[...] + norm_far[...]
    norm_dp[...] = both
    norms[d] = both
    for i in range(1, N):
        to_dp(i).start()
    slot.second()
    gather.middle(1)
    slot.third()
    gather.middle(2)
    gather.close()
    slot.close()
    for i in range(1, N):
        from_dp(i).wait_recv()
    for i in range(1, N):
        to_mp(i).wait_send()
        to_dp(i).wait_send()
    over.wait_send()


def gather_grads(gq, gk, gv, relayed, norm, slices, rights):
    small = pltpu.VMEM((8, 128), F32)
    return pl.pallas_call(
        final_kernel,
        name="gather_grads",
        out_shape=(
            jax.ShapeDtypeStruct(slices.shape, BF16),
            jax.ShapeDtypeStruct(rights.shape, BF16),
            jax.ShapeDtypeStruct((N, 8, 128), F32),
        ),
        in_specs=[VM, VM, VM, ANY, VM, HBM, HBM],
        out_specs=(HBM, HBM, VM),
        scratch_shapes=[
            pltpu.VMEM((ROWS, PIECE), BF16),
            pltpu.VMEM((N, 8, 128), F32),
            small,
            small,
            small,
            DMA((3, 8)),
            DMA((3, 8)),
            DMA((3,)),
            DMA,
            DMA,
            DMA,
            DMA((SLICE_CHUNKS, 7)),
            DMA((SLICE_CHUNKS, 7)),
            DMA((SLICE_CHUNKS,)),
            DMA((7,)),
            DMA((7,)),
            DMA,
            DMA,
            DMA((7,)),
            DMA((7,)),
        ],
        input_output_aliases={5: 0, 6: 1},
        compiler_params=pltpu.CompilerParams(collective_id=3, has_side_effects=True),
    )(gq, gk, gv, relayed, norm, slices, rights)


def dot_nt(a, b):
    return lax.dot_general(a, b, (((1,), (1,)), ((), ())), preferred_element_type=F32)


def dot_nn(a, b):
    return lax.dot_general(a, b, (((1,), (0,)), ((), ())), preferred_element_type=F32)


def dot_tn(a, b):
    return lax.dot_general(a, b, (((0,), (0,)), ((), ())), preferred_element_type=F32)


def head_masks():
    lane = lax.broadcasted_iota(jnp.int32, (128, 128), 1)
    return lane < HEAD, lane >= HEAD


def soft(q, k, mask, key_ok):
    zero = jnp.zeros_like(q)
    scores = dot_nt(jnp.where(mask, q, zero), k) * HEAD ** (-0.5)
    scores = jnp.where(key_ok, scores, -jnp.inf)
    weights = jnp.exp(scores - jnp.max(scores, axis=-1, keepdims=True))
    return weights / jnp.sum(weights, axis=-1, keepdims=True)


def attend_kernel(lens, q_ref, k_ref, v_ref, ctx_ref):
    key_ok = lax.broadcasted_iota(jnp.int32, (128, 128), 1) < lens[pl.program_id(0)]
    masks = head_masks()
    for pair in range(4):
        cols = slice(pair * 128, pair * 128 + 128)
        q, k, v = q_ref[:, cols], k_ref[:, cols], v_ref[:, cols]
        zero = jnp.zeros_like(q)
        ctx = jnp.zeros((128, 128), F32)
        for mask in masks:
            probs = soft(q, k, mask, key_ok)
            ctx = ctx + dot_nn(probs.astype(BF16), jnp.where(mask, v, zero))
        ctx_ref[:, cols] = ctx.astype(BF16)


def attend(lens, q, k, v):
    spec = pl.BlockSpec((128, PIECE), lambda e: (e, 0))
    return pl.pallas_call(
        attend_kernel,
        name="attend",
        grid=(2,),
        in_specs=[SM] + [spec] * 3,
        out_specs=spec,
        out_shape=jax.ShapeDtypeStruct((ROWS, PIECE), BF16),
    )(lens, q, k, v)


def attend_all_kernel(lens, q_ref, k_ref, v_ref, g_ref, ctx_ref, gq_ref, gk_ref, gv_ref):
    key_ok = lax.broadcasted_iota(jnp.int32, (128, 128), 1) < lens[pl.program_id(0)]
    masks = head_masks()
    for pair in range(4):
        cols = slice(pair * 128, pair * 128 + 128)
        q, k, v, g = q_ref[:, cols], k_ref[:, cols], v_ref[:, cols], g_ref[:, cols]
        zero = jnp.zeros_like(q)
        ctx = gq = gk = gv = jnp.zeros((128, 128), F32)
        for mask in masks:
            probs = soft(q, k, mask, key_ok)
            low = probs.astype(BF16)
            g_one = jnp.where(mask, g, zero)
            gp = dot_nt(g_one, v)
            inner = jnp.sum(gp * probs, axis=-1, keepdims=True)
            gs = (probs * (gp - inner) * HEAD ** (-0.5)).astype(BF16)
            ctx = ctx + dot_nn(low, jnp.where(mask, v, zero))
            gq = gq + dot_nn(gs, jnp.where(mask, k, zero))
            gk = gk + dot_tn(gs, jnp.where(mask, q, zero))
            gv = gv + dot_tn(low, g_one)
        ctx_ref[:, cols] = ctx.astype(BF16)
        gq_ref[:, cols] = gq.astype(BF16)
        gk_ref[:, cols] = gk.astype(BF16)
        gv_ref[:, cols] = gv.astype(BF16)


def attend_all(lens, q, k, v, g):
    spec = pl.BlockSpec((128, PIECE), lambda e: (e, 0))
    shape = jax.ShapeDtypeStruct((ROWS, PIECE), BF16)
    return pl.pallas_call(
        attend_all_kernel,
        name="attend_all",
        grid=(2,),
        in_specs=[SM] + [spec] * 4,
        out_specs=(spec,) * 4,
        out_shape=(shape,) * 4,
    )(lens, q, k, v, g)


def norm_kernel(sec, xa, xb, xr, gq, gk, gv, ctx, out):
    example = pl.program_id(0)
    is_dec = sec[0] == 1

    def gram(ref):
        return dot_nt(ref[...], ref[...])

    kv, cc = gram(gk) + gram(gv), gram(ctx)
    none = jnp.zeros_like(cc)
    total = gram(xa) * (gram(gq) + jnp.where(is_dec, none, kv))
    total = total + gram(xr) * jnp.where(is_dec, kv, cc) + gram(xb) * jnp.where(is_dec, cc, none)
    value = jnp.sum(total)
    lane = lax.broadcasted_iota(jnp.int32, (8, 128), 1)
    mine = jnp.where(lane == example, value, 0.0)

    @pl.when(example == 0)
    def _():
        out[...] = mine

    @pl.when(example == 1)
    def _():
        out[...] += mine


def norm_parts(sec, xa, xb, xr, gq, gk, gv, ctx):
    wide = pl.BlockSpec((128, D), lambda e: (e, 0))
    thin = pl.BlockSpec((128, PIECE), lambda e: (e, 0))
    return pl.pallas_call(
        norm_kernel,
        name="norm_parts",
        grid=(2,),
        in_specs=[SM] + [wide] * 3 + [thin] * 4,
        out_specs=pl.BlockSpec((8, 128), lambda e: (0, 0)),
        out_shape=jax.ShapeDtypeStruct((8, 128), F32),
    )(sec, xa, xb, xr, gq, gk, gv, ctx)


BLOCK = 128


def weight_kernel(sec, clip, x_ref, y_ref, noise_ref, out_ref, scaled):
    @pl.when(pl.program_id(0) == 0)
    def _():
        for mat in range(4):

            @pl.loop(0, 16)
            def _(e):
                rows = pl.ds(pl.multiple_of(e * 128, 128), 128)
                scaled[mat, rows] = (y_ref[mat, rows].astype(F32) * clip[e]).astype(BF16)

    is_dec = sec[0]
    picks = (0, 2 * is_dec, 2 * is_dec, 2 - is_dec)
    for mat in range(4):
        total = dot_tn(x_ref[picks[mat]], scaled[mat])
        out_ref[:, mat, :] = (total + noise_ref[:, mat, :]) * (1.0 / 16.0)


def weight_grads(sec, clip, slices, rights, dp_noise):
    wide = pl.BlockSpec((BLOCK, 4, PIECE), lambda b: (b, 0, 0))
    return pl.pallas_call(
        weight_kernel,
        name="weight_grads",
        grid=(PIECE // BLOCK,),
        in_specs=[
            SM,
            SM,
            pl.BlockSpec((3, N * ROWS, BLOCK), lambda b: (0, 0, b)),
            pl.BlockSpec((4, N * ROWS, PIECE), lambda b: (0, 0, 0), pipeline_mode=pl.Buffered(1)),
            wide,
        ],
        out_specs=wide,
        out_shape=jax.ShapeDtypeStruct((PIECE, 4, PIECE), F32),
        scratch_shapes=[pltpu.VMEM((4, N * ROWS, PIECE), BF16)],
    )(sec, clip, slices, rights, dp_noise)


def rms_norm(values_in, gain_row):
    value32 = values_in.astype(F32)
    inverse = lax.rsqrt(jnp.mean(value32 * value32, axis=-1, keepdims=True) + 1e-06)
    return (value32 * inverse * gain_row.astype(F32)).astype(BF16)


def project(left, right):
    return jnp.dot(left, right, preferred_element_type=F32).astype(BF16)


def back_term(left, right):
    return jnp.einsum("sj,dj->sd", left, right, preferred_element_type=F32)


def per_device(inputs, norm_gains, weights, cotangent, lengths, dp_noise):
    section = lax.axis_index("section")
    is_dec = section == 1
    sec = jnp.reshape(section, (1,)).astype(jnp.int32)
    own_inputs = inputs[0].reshape(ROWS, D)
    normed = rms_norm(own_inputs, norm_gains[0])
    positions = jnp.arange(128)
    keep = (positions[None, :] < lengths[1][:, None]).astype(BF16)
    gout = (cotangent * keep[:, :, None]).reshape(ROWS, D)
    wt = jnp.swapaxes(weights[0], 0, 1)
    full, slices = gather_weights(wt, normed, gout)
    mats = full.reshape(4, D, PIECE)
    lens = lengths[0]
    thin = jnp.zeros((ROWS, PIECE), BF16)
    wide = jnp.zeros((ROWS, D), BF16)

    def first_dec():
        return project(normed, mats[0]), thin, thin, project(gout, mats[3]), thin, wide

    def first_enc():
        q, k, v = (project(normed, mats[i]) for i in range(3))
        ctx = attend(lens, q, k, v)
        return q, k, v, thin, ctx, back_term(ctx, mats[3]).astype(BF16)

    q, k, v, gctx, ctx, terms = lax.cond(is_dec, first_dec, first_enc)
    own_piece = lax.dynamic_slice_in_dim(own_inputs, lax.axis_index("mp") * PIECE, PIECE, 1)
    relayed = relay_forward(terms, own_piece)

    def second_dec():
        k, v = project(relayed, mats[1]), project(relayed, mats[2])
        ctx, gq, gk, gv = attend_all(lens, q, k, v, gctx)
        terms = (back_term(gk, mats[1]) + back_term(gv, mats[2])).astype(BF16)
        return ctx, gq, gk, gv, terms

    def second_enc():
        return ctx, thin, thin, thin, wide

    ctx, gq, gk, gv, terms = lax.cond(is_dec, second_dec, second_enc)
    relayed, rights = relay_backward(terms, ctx, relayed)

    def third_dec():
        return gq, gk, gv

    def third_enc():
        _, gq, gk, gv = attend_all(lens, q, k, v, project(relayed, mats[3]))
        return gq, gk, gv

    gq, gk, gv = lax.cond(is_dec, third_dec, third_enc)
    norm = norm_parts(sec, normed, gout, relayed, gq, gk, gv, ctx)
    slices, rights, norms = gather_grads(gq, gk, gv, relayed, norm, slices, rights)
    sq_norm = norms[:, 0, :2]
    bound = jnp.sqrt(jnp.float32(8.0 * D * HEADS * HEAD))
    clip_all = bound / (jnp.sqrt(sq_norm) + 0.01 * bound)
    clip_scale = lax.dynamic_index_in_dim(clip_all, lax.axis_index("dp"), 0, keepdims=False)
    noisy_grad = weight_grads(sec, clip_all.reshape(16), slices, rights, dp_noise[0])
    return (noisy_grad[None], clip_scale)


def solution(mesh):
    placed = (
        P("section", "dp", None, None),
        P("section", None),
        P("section", "dp", None, "mp"),
        P("dp", None, None),
        P(None, "dp"),
        P("section", "dp", None, "mp"),
    )
    return jax.shard_map(
        per_device,
        mesh=mesh,
        in_specs=placed,
        out_specs=(P("section", "dp", None, "mp"), P("dp")),
        check_vma=False,
    )
```

```python
import functools

import jax
import jax.numpy as jnp
from jax import lax
from jax.experimental import pallas as pl
from jax.experimental.pallas import tpu as pltpu
from jax.sharding import PartitionSpec as P

D = 4096
HEADS = 64
HEAD = 64
MESH = pl.DeviceIdType.MESH
F32 = jnp.float32
BF16 = jnp.bfloat16
N = 8
ROWS = 256
PIECE = 512
CHUNKS = 8
CH = ROWS // CHUNKS
ANY = pl.BlockSpec(memory_space=pl.ANY)
HBM = pl.BlockSpec(memory_space=pltpu.HBM)
VM = pl.BlockSpec(memory_space=pltpu.VMEM)
SM = pl.BlockSpec(memory_space=pltpu.SMEM)
DMA = pltpu.SemaphoreType.DMA


def rc(src, dst, send_sem, recv_sem, dev):
    return pltpu.make_async_remote_copy(
        src_ref=src,
        dst_ref=dst,
        send_sem=send_sem,
        recv_sem=recv_sem,
        device_id=dev,
        device_id_type=MESH,
    )


def coords():
    return lax.axis_index("section"), lax.axis_index("dp"), lax.axis_index("mp")


def greet(devs, extra=None):
    barrier = pltpu.get_barrier_semaphore()
    for dev in devs:
        pl.semaphore_signal(barrier, inc=1, device_id=dev, device_id_type=MESH)
    if extra is not None:
        cond, dev = extra

        @pl.when(cond)
        def _():
            pl.semaphore_signal(barrier, inc=1, device_id=dev, device_id_type=MESH)

        pl.semaphore_wait(barrier, len(devs) + jnp.where(cond, 1, 0))
    else:
        pl.semaphore_wait(barrier, len(devs))


def mp_peers(s, d, m):
    return [(s, d, (m + i) % N) for i in range(1, N)]


def dp_near(s, d, m):
    return [(s, (d + 2) % N, m), (s, (d + 6) % N, m), (s, d + 1 - 2 * (d % 2), m)]


class DpGather:
    def __init__(self, count, own, dst, half, send, recv, local):
        self.n, self.own, self.dst, self.half = count, own, dst, half
        self.send, self.recv, self.local = send, recv, local
        s, d, m = coords()
        self.d = d
        self.left, self.right, self.far = (d + 6) % N, (d + 2) % N, (d + 4) % N
        self.sib = d + 1 - 2 * (d % 2)
        self.to_right, self.to_left = (s, self.right, m), (s, self.left, m)
        self.to_sib = (s, self.sib, m)

    def cp(self, j, kind, src, dst, dev):
        return rc(src, dst, self.send.at[j, kind], self.recv.at[j, kind], dev)

    def keep(self, j):
        return pltpu.make_async_copy(self.own(j), self.dst(j, self.d), self.local.at[j])

    def out(self, j, kind):
        d = self.d
        if kind == 0:
            return self.cp(j, 0, self.own(j), self.dst(j, d), self.to_right)
        if kind == 1:
            return self.cp(j, 1, self.own(j), self.dst(j, d), self.to_left)
        if kind == 2:
            ref = self.half(j, self.left, 0)
            return self.cp(j, 2, ref, ref, self.to_right)
        if kind == 3:
            ref = self.half(j, self.right, 1)
            return self.cp(j, 3, ref, ref, self.to_left)
        if kind == 4:
            return self.cp(j, 4, self.own(j), self.dst(j, d), self.to_sib)
        block = (self.left, self.right, self.far)[kind - 5]
        return self.cp(j, kind, self.dst(j, block), self.dst(j, block), self.to_sib)

    def into(self, j, kind):
        sib = self.sib
        if kind == 0:
            ref = self.dst(j, self.left)
        elif kind == 1:
            ref = self.dst(j, self.right)
        elif kind == 2:
            ref = self.half(j, self.far, 0)
        elif kind == 3:
            ref = self.half(j, self.far, 1)
        else:
            ref = self.dst(j, (sib, (sib + 6) % N, (sib + 2) % N, (sib + 4) % N)[kind - 4])
        return self.cp(j, kind, ref, ref, self.to_sib)

    def begin(self, j):
        self.out(j, 0).start()
        self.out(j, 1).start()
        self.out(j, 4).start()
        self.keep(j).start()

    def open(self):
        for j in range(min(2, self.n)):
            self.begin(j)

    def far_on(self, j):
        self.into(j, 2).wait_recv()
        self.into(j, 3).wait_recv()
        self.out(j, 7).start()

    def middle(self, j):
        self.into(j, 0).wait_recv()
        self.into(j, 1).wait_recv()
        self.out(j, 2).start()
        self.out(j, 3).start()
        self.out(j, 5).start()
        self.out(j, 6).start()
        if j + 2 < self.n:
            self.begin(j + 2)
        if j > 0:
            self.far_on(j - 1)

    def close(self):
        self.far_on(self.n - 1)
        for j in range(self.n):
            for kind in range(4, 8):
                self.into(j, kind).wait_recv()
            for kind in range(8):
                self.out(j, kind).wait_send()
            self.keep(j).wait()


class MpGather:
    def __init__(self, chunks, source, slot, send, recv, local):
        s, d, m = coords()
        self.chunks, self.source, self.slot = chunks, source, slot
        self.send, self.recv, self.local = send, recv, local
        x, y = m // 4, m % 4
        up, down, far = (y + 1) % 4, (y + 3) % 4, (y + 2) % 4
        self.m, self.xm = m, (1 - x) * 4 + y
        self.to = ((s, d, self.xm), (s, d, x * 4 + up), (s, d, x * 4 + down))
        self.sources = (m, m, m, self.xm, self.xm, down, 4 + up)
        self.landing = (
            self.xm,
            x * 4 + down,
            x * 4 + up,
            (1 - x) * 4 + down,
            (1 - x) * 4 + up,
            far,
            4 + far,
        )

    def out(self, c, kind):
        dest = self.slot(self.sources[kind], c)
        src = self.source(c) if kind < 3 else dest
        to = self.to[(0, 1, 2, 1, 2, 1, 2)[kind]]
        return rc(src, dest, self.send.at[c, kind], self.recv.at[c, kind], to)

    def into(self, c, kind):
        ref = self.slot(self.landing[kind], c)
        return rc(ref, ref, self.send.at[c, kind], self.recv.at[c, kind], self.to[0])

    def keep(self, c):
        return pltpu.make_async_copy(self.source(c), self.slot(self.m, c), self.local.at[c])

    def stage(self, c, number):
        if not 0 <= c < self.chunks:
            return
        waits, starts = (((), (0, 1, 2)), ((0,), (3, 4)), ((1, 2, 3, 4), (5, 6)), ((5, 6), ()))[number]
        for kind in waits:
            self.into(c, kind).wait_recv()
        for kind in starts:
            self.out(c, kind).start()
        if number == 0:
            self.keep(c).start()
        if number == 3:
            self.keep(c).wait()

    def close(self):
        for c in range(self.chunks):
            for kind in range(7):
                self.out(c, kind).wait_send()


def mp_near(s, d, m):
    x, y = m // 4, m % 4
    return [(s, d, (1 - x) * 4 + y), (s, d, x * 4 + (y + 1) % 4), (s, d, x * 4 + (y + 3) % 4)]


SLICE_CHUNKS = 2


class SliceGather:
    def __init__(self, source, turn, dest, send_t, recv_t, local_t, send, recv, local):
        s, d, m = coords()
        self.d, self.m = d, m
        self.far = lambda: rc(source, turn, send_t, recv_t, (s, m, d))
        self.near = lambda: pltpu.make_async_copy(source, turn, local_t)
        step = ROWS // SLICE_CHUNKS
        self.gather = MpGather(
            SLICE_CHUNKS,
            lambda c: turn.at[pl.ds(c * step, step)],
            lambda mm, c: dest.at[pl.ds(pl.multiple_of(mm * ROWS + c * step, step), step)],
            send,
            recv,
            local,
        )

    def open(self):
        pl.when(self.d != self.m)(lambda: self.far().start())
        pl.when(self.d == self.m)(lambda: self.near().start())

    def middle(self):
        pl.when(self.d != self.m)(lambda: self.far().wait_recv())
        pl.when(self.d == self.m)(lambda: self.near().wait())
        for c in range(SLICE_CHUNKS):
            self.gather.stage(c, 0)

    def second(self):
        for c in range(SLICE_CHUNKS):
            self.gather.stage(c, 1)

    def third(self):
        for c in range(SLICE_CHUNKS):
            self.gather.stage(c, 2)

    def close(self):
        for c in range(SLICE_CHUNKS):
            self.gather.stage(c, 3)
        self.gather.close()
        pl.when(self.d != self.m)(lambda: self.far().wait_send())


def piece(ref, m, rows=None):
    cols = pl.ds(pl.multiple_of(m * PIECE, PIECE), PIECE)
    if rows is None:
        return ref.at[:, cols]
    return ref.at[pl.ds(rows, CH), cols]


def gather_kernel(wt, xa, xb, full, slices, turn, w_send, w_recv, w_loc, t_send, t_recv, t_loc, b_send, b_recv, b_loc):
    s, d, m = coords()
    greet(mp_near(s, d, m) + dp_near(s, d, m), (d != m, (s, m, d)))
    gather = DpGather(
        4,
        lambda j: wt.at[j],
        lambda j, b: full.at[j, b],
        lambda j, b, h: full.at[j, b, pl.ds(h * 256, 256)],
        w_send,
        w_recv,
        w_loc,
    )
    slots = [
        SliceGather(
            piece(ref, m),
            turn.at[i],
            slices.at[i],
            t_send.at[i],
            t_recv.at[i],
            t_loc.at[i],
            b_send.at[i],
            b_recv.at[i],
            b_loc.at[i],
        )
        for i, ref in enumerate((xa, xb))
    ]
    gather.open()
    slots[0].open()
    pl.when(s == 1)(slots[1].open)
    slots[0].middle()
    pl.when(s == 1)(slots[1].middle)
    gather.middle(0)
    slots[0].second()
    pl.when(s == 1)(slots[1].second)
    gather.middle(1)
    slots[0].third()
    pl.when(s == 1)(slots[1].third)
    for j in range(2, 4):
        gather.middle(j)
    gather.close()
    slots[0].close()
    pl.when(s == 1)(slots[1].close)


def gather_weights(wt, xa, xb):
    return pl.pallas_call(
        gather_kernel,
        name="gather_weights",
        out_shape=(
            jax.ShapeDtypeStruct((4, N, PIECE, PIECE), BF16),
            jax.ShapeDtypeStruct((3, N * ROWS, PIECE), BF16),
        ),
        in_specs=[VM, ANY, ANY],
        out_specs=(HBM, HBM),
        scratch_shapes=[
            pltpu.VMEM((2, ROWS, PIECE), BF16),
            DMA((4, 8)),
            DMA((4, 8)),
            DMA((4,)),
            DMA((2,)),
            DMA((2,)),
            DMA((2,)),
            DMA((2, SLICE_CHUNKS, 7)),
            DMA((2, SLICE_CHUNKS, 7)),
            DMA((2, SLICE_CHUNKS)),
        ],
        compiler_params=pltpu.CompilerParams(collective_id=0, has_side_effects=True),
    )(wt, xa, xb)


class Relay:
    def __init__(self, terms, resid, total, bufs, sems):
        self.terms, self.resid = terms, resid
        (self.one, self.direct, self.passed, self.mixed, self.kept, self.cross, self.over, self.summed, self.landed) = bufs
        self.send, self.recv, g_send, g_recv, g_loc = sems
        s, d, m = coords()
        x, y = m // 4, m % 4
        self.x, self.y, self.m = x, y, m
        self.up, self.down, self.opp = (y + 1) % 4, (y + 3) % 4, (y + 2) % 4
        self.to_up, self.to_down = (s, d, x * 4 + self.up), (s, d, x * 4 + self.down)
        self.to_x = (s, d, (1 - x) * 4 + y)
        self.partner = (1 - s, d, (1 - x) * 4 + y)
        self.gather = MpGather(
            CHUNKS,
            lambda c: self.landed.at[self.rows(c)],
            lambda mm, c: piece(total, (mm + 4) % N, c * CH),
            g_send,
            g_recv,
            g_loc,
        )

    def rows(self, c):
        return pl.ds(c * CH, CH)

    def cp(self, c, kind, src, dst, to):
        return rc(src, dst, self.send.at[c, kind], self.recv.at[c, kind], to)

    def copy(self, c, kind):
        rows = self.rows(c)
        return (
            lambda: self.cp(c, 0, piece(self.terms, self.opp, c * CH), self.one.at[0, rows], self.to_up),
            lambda: self.cp(c, 1, piece(self.terms, 4 + self.opp, c * CH), self.one.at[1, rows], self.to_down),
            lambda: self.cp(c, 2, piece(self.terms, 4 + self.up, c * CH), self.direct.at[1, rows], self.to_up),
            lambda: self.cp(c, 3, piece(self.terms, self.down, c * CH), self.direct.at[0, rows], self.to_down),
            lambda: self.cp(c, 4, self.mixed.at[0, rows], self.passed.at[0, rows], self.to_up),
            lambda: self.cp(c, 5, self.mixed.at[1, rows], self.passed.at[1, rows], self.to_down),
            lambda: self.cp(c, 6, self.cross.at[rows], self.over.at[rows], self.to_x),
            lambda: self.cp(c, 7, self.summed.at[rows], self.landed.at[rows], self.partner),
        )[kind]()

    def mine(self, index, c):
        return self.terms[pl.ds(c * CH, CH), pl.ds(pl.multiple_of(index * PIECE, PIECE), PIECE)].astype(F32)

    def stage(self, c, number):
        if not 0 <= c < CHUNKS:
            return
        rows = self.rows(c)
        if number == 1:
            for side, index in ((0, self.up), (1, 4 + self.down)):
                self.copy(c, side).wait_recv()
                value = self.one[side, rows].astype(F32) + self.mine(index, c)
                self.mixed[side, rows] = value.astype(BF16)
                self.copy(c, 4 + side).start()
            for kind in (2, 3):
                self.copy(c, kind).start()
        elif number == 2:
            for kind in range(2, 6):
                self.copy(c, kind).wait_recv()
            for side in range(2):
                value = self.direct[side, rows].astype(F32) + self.passed[side, rows].astype(F32)
                value = value + self.mine(side * 4 + self.y, c)

                @pl.when(self.x == side)
                def _():
                    self.kept[rows] = value

                @pl.when(self.x != side)
                def _():
                    self.cross[rows] = value.astype(BF16)

            self.copy(c, 6).start()
        else:
            self.copy(c, 6).wait_recv()
            value = self.kept[rows] + self.over[rows].astype(F32)
            if self.with_resid:
                value = value + self.resid[rows].astype(F32)
            self.summed[rows] = value.astype(BF16)
            self.copy(c, 7).start()

    def sender_open(self):
        for c in range(CHUNKS):
            for kind in range(2):
                self.copy(c, kind).start()

    def sender(self, with_resid):
        self.with_resid = with_resid
        for tick in range(CHUNKS + 2):
            for number in range(1, 4):
                self.stage(tick + 1 - number, number)

    def sender_close(self):
        for c in range(CHUNKS):
            for kind in range(8):
                self.copy(c, kind).wait_send()

    def taker(self):
        for tick in range(CHUNKS + 3):
            if tick < CHUNKS:
                self.copy(tick, 7).wait_recv()
            for number in range(4):
                self.gather.stage(tick - number, number)


SIDES = pltpu.VMEM((2, ROWS, PIECE), BF16)
ONE = pltpu.VMEM((ROWS, PIECE), BF16)
RELAY_BUFS = [SIDES, SIDES, SIDES, SIDES, pltpu.VMEM((ROWS, PIECE), F32), ONE, ONE, ONE, ONE]
RELAY_SEMS = [DMA((CHUNKS, 8)), DMA((CHUNKS, 8)), DMA((CHUNKS, 7)), DMA((CHUNKS, 7)), DMA((CHUNKS,))]


def bridge_kernel(
    lens, q_ref, k_in, v_in, g_in, resid, xa, xb, mats, ctx_ref, gq_ref, gk_ref, gv_ref, total, norm, rights, *rest
):
    s, d, m = coords()
    greet(mp_near(s, d, m) + dp_near(s, d, m) + [(1 - s, d, (m + 4) % N)])
    bufs, sems = rest[:9], rest[9:14]
    y_send, y_recv, y_loc, w_sem, wbuf, terms, k_mid, v_mid, g_mid, gram_a, gram_b = rest[14:]
    relay = Relay(terms, resid, total, bufs, sems)
    gather = DpGather(
        1,
        lambda j: ctx_ref,
        lambda j, b: rights.at[3, pl.ds(pl.multiple_of(b * ROWS, ROWS), ROWS)],
        lambda j, b, h: rights.at[3, pl.ds(pl.multiple_of(b * ROWS + h * 128, 128), 128)],
        y_send,
        y_recv,
        y_loc,
    )

    def load(mat, slot):
        return pltpu.make_async_copy(mats.at[mat], wbuf.at[slot], w_sem.at[slot])

    def block(slot, index):
        return wbuf[slot, pl.ds(pl.multiple_of(index * PIECE, PIECE), PIECE)]

    def put(index, value):
        terms[:, pl.ds(pl.multiple_of(index * PIECE, PIECE), PIECE)] = value.astype(BF16)

    def send_terms(term):
        for group in ((relay.opp, 4 + relay.opp), (relay.up, 4 + relay.down, 4 + relay.up, relay.down)):
            for index in group:
                put(index, term(index))
            if group[0] is relay.opp:
                relay.sender_open()
        for index in (relay.y, 4 + relay.y):
            put(index, term(index))

    def grams(src, dst):
        for e in range(2):
            rows = src[pl.ds(e * 128, 128)]
            dst[e] = dot_nt(rows, rows)

    def thin_gram(ref, e):
        rows = ref[pl.ds(e * 128, 128)]
        return dot_nt(rows, rows)

    def note(value_of):
        lane = lax.broadcasted_iota(jnp.int32, (8, 128), 1)
        norm[...] = jnp.where(lane == 0, jnp.sum(value_of(0)), 0.0) + jnp.where(lane == 1, jnp.sum(value_of(1)), 0.0)

    def wide_dot(left, slot, out):
        for half in range(2):
            cols = slice(half * 256, half * 256 + 256)
            out[:, cols] = dot_nn(left[...], wbuf[slot, :, cols]).astype(BF16)

    def each_head(body):
        @pl.loop(0, 2)
        def _(e):
            rows = pl.ds(pl.multiple_of(e * 128, 128), 128)
            key_ok = lax.broadcasted_iota(jnp.int32, (128, 128), 1) < lens[e]
            for pair in range(4):
                body(rows, slice(pair * 128, pair * 128 + 128), key_ok)

    @pl.when(s == 0)
    def _():
        load(3, 0).start()

        def ahead(rows, cols, key_ok):
            ctx_ref[rows, cols] = context(q_ref[rows, cols], k_in[rows, cols], v_in[rows, cols], key_ok)

        each_head(ahead)
        gather.open()
        load(3, 0).wait()
        send_terms(lambda index: dot_nt(ctx_ref[...], block(0, index)))
        relay.sender(True)
        gather.middle(0)
        grams(xa, gram_a)
        gather.close()
        relay.taker()
        wide_dot(total, 0, g_mid)

        def back(rows, cols, key_ok):
            _, gq, gk, gv = gradients(
                q_ref[rows, cols], k_in[rows, cols], v_in[rows, cols], g_mid[rows, cols], key_ok, False
            )
            gq_ref[rows, cols], gk_ref[rows, cols], gv_ref[rows, cols] = gq, gk, gv

        each_head(back)
        grams(total, gram_b)
        note(
            lambda e: gram_a[e] * (thin_gram(gq_ref, e) + thin_gram(gk_ref, e) + thin_gram(gv_ref, e))
            + gram_b[e] * thin_gram(ctx_ref, e)
        )
        relay.sender_close()
        relay.gather.close()

    @pl.when(s == 1)
    def _():
        load(1, 0).start()
        load(2, 1).start()
        grams(xa, gram_a)
        grams(xb, gram_b)
        load(1, 0).wait()
        load(2, 1).wait()
        relay.taker()
        wide_dot(total, 0, k_mid)
        wide_dot(total, 1, v_mid)

        def both(rows, cols, key_ok):
            ctx, gq, gk, gv = gradients(
                q_ref[rows, cols], k_mid[rows, cols], v_mid[rows, cols], g_in[rows, cols], key_ok, True
            )
            ctx_ref[rows, cols], gq_ref[rows, cols], gk_ref[rows, cols], gv_ref[rows, cols] = ctx, gq, gk, gv

        each_head(both)
        send_terms(lambda index: dot_nt(gk_ref[...], block(0, index)) + dot_nt(gv_ref[...], block(1, index)))
        gather.open()
        relay.sender(False)
        gather.middle(0)

        def value_of(e):
            rows = total[pl.ds(e * 128, 128)]
            return (
                gram_a[e] * thin_gram(gq_ref, e)
                + dot_nt(rows, rows) * (thin_gram(gk_ref, e) + thin_gram(gv_ref, e))
                + gram_b[e] * thin_gram(ctx_ref, e)
            )

        note(value_of)
        gather.close()
        relay.sender_close()
        relay.gather.close()


def bridge(lens, q, k, v, g, resid, xa, xb, mats):
    thin = jax.ShapeDtypeStruct((ROWS, PIECE), BF16)
    small = pltpu.VMEM((ROWS, PIECE), BF16)
    return pl.pallas_call(
        bridge_kernel,
        name="bridge",
        out_shape=(thin,) * 4
        + (
            jax.ShapeDtypeStruct((ROWS, D), BF16),
            jax.ShapeDtypeStruct((8, 128), F32),
            jax.ShapeDtypeStruct((4, N * ROWS, PIECE), BF16),
        ),
        in_specs=[SM] + [VM] * 7 + [HBM],
        out_specs=(VM,) * 6 + (HBM,),
        scratch_shapes=RELAY_BUFS
        + RELAY_SEMS
        + [
            DMA((1, 8)),
            DMA((1, 8)),
            DMA((1,)),
            DMA((2,)),
            pltpu.VMEM((2, D, PIECE), BF16),
            pltpu.VMEM((ROWS, D), BF16),
            small,
            small,
            small,
            pltpu.VMEM((2, 128, 128), F32),
            pltpu.VMEM((2, 128, 128), F32),
        ],
        compiler_params=pltpu.CompilerParams(collective_id=1, has_side_effects=True),
    )(lens, q, k, v, g, resid, xa, xb, mats)


def final_kernel(
    gq, gk, gv, relayed, norm, slices_in, rights_in, slices, rights, norms,
    turn, norm_mp, norm_own, norm_far, norm_dp,
    y_send, y_recv, y_loc, t_send, t_recv, t_loc, b_send, b_recv, b_loc, n_send, n_recv, f_send, f_recv, e_send, e_recv,
):
    s, d, m = coords()
    dp_all = [(s, (d + i) % N, m) for i in range(1, N)]
    greet(mp_peers(s, d, m) + dp_all + [(1 - s, d, m)], (d != m, (s, m, d)))
    parts = (gq, gk, gv)
    gather = DpGather(
        3,
        lambda j: parts[j],
        lambda j, b: rights.at[j, pl.ds(pl.multiple_of(b * ROWS, ROWS), ROWS)],
        lambda j, b, h: rights.at[j, pl.ds(pl.multiple_of(b * ROWS + h * 128, 128), 128)],
        y_send,
        y_recv,
        y_loc,
    )
    slot = SliceGather(
        piece(relayed, m), turn, slices.at[2], t_send, t_recv, t_loc, b_send, b_recv, b_loc
    )

    def to_mp(i):
        return rc(norm, norm_mp.at[m], n_send.at[i - 1], n_recv.at[i - 1], (s, d, (m + i) % N))

    def from_mp(i):
        ref = norm_mp.at[(m + N - i) % N]
        return rc(ref, ref, n_send.at[i - 1], n_recv.at[i - 1], (s, d, (m + i) % N))

    def to_dp(i):
        return rc(norm_dp, norms.at[d], e_send.at[i - 1], e_recv.at[i - 1], (s, (d + i) % N, m))

    def from_dp(i):
        ref = norms.at[(d + N - i) % N]
        return rc(ref, ref, e_send.at[i - 1], e_recv.at[i - 1], (s, (d + i) % N, m))

    slot.open()
    for i in range(1, N):
        to_mp(i).start()
    gather.open()
    norm_mp[m] = norm[...]
    for i in range(1, N):
        from_mp(i).wait_recv()
    acc = norm_mp[0]
    for i in range(1, N):
        acc = acc + norm_mp[i]
    norm_own[...] = acc
    over = rc(norm_own, norm_far, f_send, f_recv, (1 - s, d, m))
    over.start()
    slot.middle()
    gather.middle(0)
    slot.second()
    over.wait_recv()
    both = norm_own[...] + norm_far[...]
    norm_dp[...] = both
    norms[d] = both
    for i in range(1, N):
        to_dp(i).start()
    slot.third()
    gather.middle(1)
    gather.middle(2)
    gather.close()
    slot.close()
    for i in range(1, N):
        from_dp(i).wait_recv()
    for i in range(1, N):
        to_mp(i).wait_send()
        to_dp(i).wait_send()
    over.wait_send()


def gather_grads(gq, gk, gv, relayed, norm, slices, rights):
    small = pltpu.VMEM((8, 128), F32)
    return pl.pallas_call(
        final_kernel,
        name="gather_grads",
        out_shape=(
            jax.ShapeDtypeStruct(slices.shape, BF16),
            jax.ShapeDtypeStruct(rights.shape, BF16),
            jax.ShapeDtypeStruct((N, 8, 128), F32),
        ),
        in_specs=[VM, VM, VM, ANY, VM, HBM, HBM],
        out_specs=(HBM, HBM, VM),
        scratch_shapes=[
            pltpu.VMEM((ROWS, PIECE), BF16),
            pltpu.VMEM((N, 8, 128), F32),
            small,
            small,
            small,
            DMA((3, 8)),
            DMA((3, 8)),
            DMA((3,)),
            DMA,
            DMA,
            DMA,
            DMA((SLICE_CHUNKS, 7)),
            DMA((SLICE_CHUNKS, 7)),
            DMA((SLICE_CHUNKS,)),
            DMA((7,)),
            DMA((7,)),
            DMA,
            DMA,
            DMA((7,)),
            DMA((7,)),
        ],
        input_output_aliases={5: 0, 6: 1},
        compiler_params=pltpu.CompilerParams(collective_id=3, has_side_effects=True),
    )(gq, gk, gv, relayed, norm, slices, rights)


def dot_nt(a, b):
    return lax.dot_general(a, b, (((1,), (1,)), ((), ())), preferred_element_type=F32)


def dot_nn(a, b):
    return lax.dot_general(a, b, (((1,), (0,)), ((), ())), preferred_element_type=F32)


def dot_tn(a, b):
    return lax.dot_general(a, b, (((0,), (0,)), ((), ())), preferred_element_type=F32)


def head_masks():
    lane = lax.broadcasted_iota(jnp.int32, (128, 128), 1)
    return lane < HEAD, lane >= HEAD


def soft(q, k, mask, key_ok):
    zero = jnp.zeros_like(q)
    scores = dot_nt(jnp.where(mask, q, zero), k) * HEAD ** (-0.5)
    scores = jnp.where(key_ok, scores, -jnp.inf)
    weights = jnp.exp(scores - jnp.max(scores, axis=-1, keepdims=True))
    return weights / jnp.sum(weights, axis=-1, keepdims=True)


def context(q, k, v, key_ok):
    zero = jnp.zeros_like(q)
    ctx = jnp.zeros((128, 128), F32)
    for mask in head_masks():
        probs = soft(q, k, mask, key_ok)
        ctx = ctx + dot_nn(probs.astype(BF16), jnp.where(mask, v, zero))
    return ctx.astype(BF16)


def gradients(q, k, v, g, key_ok, with_context):
    zero = jnp.zeros_like(q)
    ctx = gq = gk = gv = jnp.zeros((128, 128), F32)
    for mask in head_masks():
        probs = soft(q, k, mask, key_ok)
        low = probs.astype(BF16)
        g_one = jnp.where(mask, g, zero)
        gp = dot_nt(g_one, v)
        inner = jnp.sum(gp * probs, axis=-1, keepdims=True)
        gs = (probs * (gp - inner) * HEAD ** (-0.5)).astype(BF16)
        if with_context:
            ctx = ctx + dot_nn(low, jnp.where(mask, v, zero))
        gq = gq + dot_nn(gs, jnp.where(mask, k, zero))
        gk = gk + dot_tn(gs, jnp.where(mask, q, zero))
        gv = gv + dot_tn(low, g_one)
    return tuple(value.astype(BF16) for value in (ctx, gq, gk, gv))


BLOCK = 128


def weight_kernel(sec, clip, x_ref, y_ref, noise_ref, out_ref, scaled):
    @pl.when(pl.program_id(0) == 0)
    def _():
        for mat in range(4):

            @pl.loop(0, 16)
            def _(e):
                rows = pl.ds(pl.multiple_of(e * 128, 128), 128)
                scaled[mat, rows] = (y_ref[mat, rows].astype(F32) * clip[e]).astype(BF16)

    is_dec = sec[0]
    picks = (0, 2 * is_dec, 2 * is_dec, 2 - is_dec)
    for mat in range(4):
        total = dot_tn(x_ref[picks[mat]], scaled[mat])
        out_ref[:, mat, :] = (total + noise_ref[:, mat, :]) * (1.0 / 16.0)


def weight_grads(sec, clip, slices, rights, dp_noise):
    wide = pl.BlockSpec((BLOCK, 4, PIECE), lambda b: (b, 0, 0))
    return pl.pallas_call(
        weight_kernel,
        name="weight_grads",
        grid=(PIECE // BLOCK,),
        in_specs=[
            SM,
            SM,
            pl.BlockSpec((3, N * ROWS, BLOCK), lambda b: (0, 0, b)),
            pl.BlockSpec((4, N * ROWS, PIECE), lambda b: (0, 0, 0), pipeline_mode=pl.Buffered(1)),
            wide,
        ],
        out_specs=wide,
        out_shape=jax.ShapeDtypeStruct((PIECE, 4, PIECE), F32),
        scratch_shapes=[pltpu.VMEM((4, N * ROWS, PIECE), BF16)],
    )(sec, clip, slices, rights, dp_noise)


def rms_norm(values_in, gain_row):
    value32 = values_in.astype(F32)
    inverse = lax.rsqrt(jnp.mean(value32 * value32, axis=-1, keepdims=True) + 1e-06)
    return (value32 * inverse * gain_row.astype(F32)).astype(BF16)


def project(left, right):
    return jnp.dot(left, right, preferred_element_type=F32).astype(BF16)


def per_device(inputs, norm_gains, weights, cotangent, lengths, dp_noise):
    section = lax.axis_index("section")
    is_dec = section == 1
    sec = jnp.reshape(section, (1,)).astype(jnp.int32)
    own_inputs = inputs[0].reshape(ROWS, D)
    normed = rms_norm(own_inputs, norm_gains[0])
    positions = jnp.arange(128)
    keep = (positions[None, :] < lengths[1][:, None]).astype(BF16)
    gout = (cotangent * keep[:, :, None]).reshape(ROWS, D)
    wt = jnp.swapaxes(weights[0], 0, 1)
    full, slices = gather_weights(wt, normed, gout)
    mats = full.reshape(4, D, PIECE)
    lens = lengths[0]
    thin = jnp.zeros((ROWS, PIECE), BF16)

    def first_dec():
        return project(normed, mats[0]), thin, thin, project(gout, mats[3])

    def first_enc():
        q, k, v = (project(normed, mats[i]) for i in range(3))
        return q, k, v, thin

    q, k, v, gctx = lax.cond(is_dec, first_dec, first_enc)
    own_piece = lax.dynamic_slice_in_dim(own_inputs, lax.axis_index("mp") * PIECE, PIECE, 1)
    ctx, gq, gk, gv, relayed, norm, rights = bridge(lens, q, k, v, gctx, own_piece, normed, gout, mats)
    slices, rights, norms = gather_grads(gq, gk, gv, relayed, norm, slices, rights)
    sq_norm = norms[:, 0, :2]
    bound = jnp.sqrt(jnp.float32(8.0 * D * HEADS * HEAD))
    clip_all = bound / (jnp.sqrt(sq_norm) + 0.01 * bound)
    clip_scale = lax.dynamic_index_in_dim(clip_all, lax.axis_index("dp"), 0, keepdims=False)
    noisy_grad = weight_grads(sec, clip_all.reshape(16), slices, rights, dp_noise[0])
    return (noisy_grad[None], clip_scale)


def solution(mesh):
    placed = (
        P("section", "dp", None, None),
        P("section", None),
        P("section", "dp", None, "mp"),
        P("dp", None, None),
        P(None, "dp"),
        P("section", "dp", None, "mp"),
    )
    return jax.shard_map(
        per_device,
        mesh=mesh,
        in_specs=placed,
        out_specs=(P("section", "dp", None, "mp"), P("dp")),
        check_vma=False,
    )
```

```python
import functools

import jax
import jax.numpy as jnp
from jax import lax
from jax.experimental import pallas as pl
from jax.experimental.pallas import tpu as pltpu
from jax.sharding import PartitionSpec as P

D = 4096
HEADS = 64
HEAD = 64
MESH = pl.DeviceIdType.MESH
F32 = jnp.float32
BF16 = jnp.bfloat16
N = 8
ROWS = 256
PIECE = 512
CHUNKS = 8
CH = ROWS // CHUNKS
ANY = pl.BlockSpec(memory_space=pl.ANY)
HBM = pl.BlockSpec(memory_space=pltpu.HBM)
VM = pl.BlockSpec(memory_space=pltpu.VMEM)
SM = pl.BlockSpec(memory_space=pltpu.SMEM)
DMA = pltpu.SemaphoreType.DMA


def rc(src, dst, send_sem, recv_sem, dev):
    return pltpu.make_async_remote_copy(
        src_ref=src,
        dst_ref=dst,
        send_sem=send_sem,
        recv_sem=recv_sem,
        device_id=dev,
        device_id_type=MESH,
    )


def coords():
    return lax.axis_index("section"), lax.axis_index("dp"), lax.axis_index("mp")


def greet(devs, extra=None):
    barrier = pltpu.get_barrier_semaphore()
    for dev in devs:
        pl.semaphore_signal(barrier, inc=1, device_id=dev, device_id_type=MESH)
    if extra is not None:
        cond, dev = extra

        @pl.when(cond)
        def _():
            pl.semaphore_signal(barrier, inc=1, device_id=dev, device_id_type=MESH)

        pl.semaphore_wait(barrier, len(devs) + jnp.where(cond, 1, 0))
    else:
        pl.semaphore_wait(barrier, len(devs))


def mp_peers(s, d, m):
    return [(s, d, (m + i) % N) for i in range(1, N)]


def dp_near(s, d, m):
    return [(s, (d + 2) % N, m), (s, (d + 6) % N, m), (s, d + 1 - 2 * (d % 2), m)]


class DpGather:
    def __init__(self, count, own, dst, half, send, recv, local):
        self.n, self.own, self.dst, self.half = count, own, dst, half
        self.send, self.recv, self.local = send, recv, local
        s, d, m = coords()
        self.d = d
        self.left, self.right, self.far = (d + 6) % N, (d + 2) % N, (d + 4) % N
        self.sib = d + 1 - 2 * (d % 2)
        self.to_right, self.to_left = (s, self.right, m), (s, self.left, m)
        self.to_sib = (s, self.sib, m)

    def cp(self, j, kind, src, dst, dev):
        return rc(src, dst, self.send.at[j, kind], self.recv.at[j, kind], dev)

    def keep(self, j):
        return pltpu.make_async_copy(self.own(j), self.dst(j, self.d), self.local.at[j])

    def out(self, j, kind):
        d = self.d
        if kind == 0:
            return self.cp(j, 0, self.own(j), self.dst(j, d), self.to_right)
        if kind == 1:
            return self.cp(j, 1, self.own(j), self.dst(j, d), self.to_left)
        if kind == 2:
            ref = self.half(j, self.left, 0)
            return self.cp(j, 2, ref, ref, self.to_right)
        if kind == 3:
            ref = self.half(j, self.right, 1)
            return self.cp(j, 3, ref, ref, self.to_left)
        if kind == 4:
            return self.cp(j, 4, self.own(j), self.dst(j, d), self.to_sib)
        block = (self.left, self.right, self.far)[kind - 5]
        return self.cp(j, kind, self.dst(j, block), self.dst(j, block), self.to_sib)

    def into(self, j, kind):
        sib = self.sib
        if kind == 0:
            ref = self.dst(j, self.left)
        elif kind == 1:
            ref = self.dst(j, self.right)
        elif kind == 2:
            ref = self.half(j, self.far, 0)
        elif kind == 3:
            ref = self.half(j, self.far, 1)
        else:
            ref = self.dst(j, (sib, (sib + 6) % N, (sib + 2) % N, (sib + 4) % N)[kind - 4])
        return self.cp(j, kind, ref, ref, self.to_sib)

    def begin(self, j):
        self.out(j, 0).start()
        self.out(j, 1).start()
        self.out(j, 4).start()
        self.keep(j).start()

    def open(self):
        for j in range(min(2, self.n)):
            self.begin(j)

    def far_on(self, j):
        self.into(j, 2).wait_recv()
        self.into(j, 3).wait_recv()
        self.out(j, 7).start()

    def middle(self, j):
        self.into(j, 0).wait_recv()
        self.into(j, 1).wait_recv()
        self.out(j, 2).start()
        self.out(j, 3).start()
        self.out(j, 5).start()
        self.out(j, 6).start()
        if j + 2 < self.n:
            self.begin(j + 2)
        if j > 0:
            self.far_on(j - 1)

    def finish(self, j):
        for kind in range(4, 8):
            self.into(j, kind).wait_recv()
        self.keep(j).wait()

    def close(self, finished=0):
        self.far_on(self.n - 1)
        for j in range(finished, self.n):
            self.finish(j)
        for j in range(self.n):
            for kind in range(8):
                self.out(j, kind).wait_send()


class MpGather:
    def __init__(self, chunks, source, slot, send, recv, local):
        s, d, m = coords()
        self.chunks, self.source, self.slot = chunks, source, slot
        self.send, self.recv, self.local = send, recv, local
        x, y = m // 4, m % 4
        up, down, far = (y + 1) % 4, (y + 3) % 4, (y + 2) % 4
        self.m, self.xm = m, (1 - x) * 4 + y
        self.to = ((s, d, self.xm), (s, d, x * 4 + up), (s, d, x * 4 + down))
        self.sources = (m, m, m, self.xm, self.xm, down, 4 + up)
        self.landing = (
            self.xm,
            x * 4 + down,
            x * 4 + up,
            (1 - x) * 4 + down,
            (1 - x) * 4 + up,
            far,
            4 + far,
        )

    def out(self, c, kind):
        dest = self.slot(self.sources[kind], c)
        src = self.source(c) if kind < 3 else dest
        to = self.to[(0, 1, 2, 1, 2, 1, 2)[kind]]
        return rc(src, dest, self.send.at[c, kind], self.recv.at[c, kind], to)

    def into(self, c, kind):
        ref = self.slot(self.landing[kind], c)
        return rc(ref, ref, self.send.at[c, kind], self.recv.at[c, kind], self.to[0])

    def keep(self, c):
        return pltpu.make_async_copy(self.source(c), self.slot(self.m, c), self.local.at[c])

    def stage(self, c, number):
        if not 0 <= c < self.chunks:
            return
        waits, starts = (((), (0, 1, 2)), ((0,), (3, 4)), ((1, 2, 3, 4), (5, 6)), ((5, 6), ()))[number]
        for kind in waits:
            self.into(c, kind).wait_recv()
        for kind in starts:
            self.out(c, kind).start()
        if number == 0:
            self.keep(c).start()
        if number == 3:
            self.keep(c).wait()

    def close(self):
        for c in range(self.chunks):
            for kind in range(7):
                self.out(c, kind).wait_send()


def mp_near(s, d, m):
    x, y = m // 4, m % 4
    return [(s, d, (1 - x) * 4 + y), (s, d, x * 4 + (y + 1) % 4), (s, d, x * 4 + (y + 3) % 4)]


SLICE_CHUNKS = 2


class SliceGather:
    def __init__(self, source, turn, dest, send_t, recv_t, local_t, send, recv, local):
        s, d, m = coords()
        self.d, self.m = d, m
        self.far = lambda: rc(source, turn, send_t, recv_t, (s, m, d))
        self.near = lambda: pltpu.make_async_copy(source, turn, local_t)
        step = ROWS // SLICE_CHUNKS
        self.gather = MpGather(
            SLICE_CHUNKS,
            lambda c: turn.at[pl.ds(c * step, step)],
            lambda mm, c: dest.at[pl.ds(pl.multiple_of(mm * ROWS + c * step, step), step)],
            send,
            recv,
            local,
        )

    def open(self):
        pl.when(self.d != self.m)(lambda: self.far().start())
        pl.when(self.d == self.m)(lambda: self.near().start())

    def middle(self):
        pl.when(self.d != self.m)(lambda: self.far().wait_recv())
        pl.when(self.d == self.m)(lambda: self.near().wait())
        for c in range(SLICE_CHUNKS):
            self.gather.stage(c, 0)

    def second(self):
        for c in range(SLICE_CHUNKS):
            self.gather.stage(c, 1)

    def third(self):
        for c in range(SLICE_CHUNKS):
            self.gather.stage(c, 2)

    def close(self):
        for c in range(SLICE_CHUNKS):
            self.gather.stage(c, 3)
        self.gather.close()
        pl.when(self.d != self.m)(lambda: self.far().wait_send())


def piece(ref, m, rows=None):
    cols = pl.ds(pl.multiple_of(m * PIECE, PIECE), PIECE)
    if rows is None:
        return ref.at[:, cols]
    return ref.at[pl.ds(rows, CH), cols]


def gather_kernel(wt, rows_in, gain, full, normed, q_ref, k_ref, v_ref, wbuf, w_sem, w_send, w_recv, w_loc):
    s, d, m = coords()
    greet(dp_near(s, d, m))
    gather = DpGather(
        4,
        lambda j: wt.at[j],
        lambda j, b: full.at[j, b],
        lambda j, b, h: full.at[j, b, pl.ds(h * 256, 256)],
        w_send,
        w_recv,
        w_loc,
    )
    gather.open()

    @pl.loop(0, ROWS // 32)
    def _(i):
        rows = pl.ds(pl.multiple_of(i * 32, 32), 32)
        value = rows_in[rows].astype(F32)
        inverse = lax.rsqrt(jnp.mean(value * value, axis=-1, keepdims=True) + 1e-06)
        normed[rows] = (value * inverse * gain[...].astype(F32)).astype(BF16)

    outs = (q_ref, k_ref, v_ref)

    def load(j):
        return pltpu.make_async_copy(full.at[j], wbuf.at[j % 2], w_sem.at[j % 2])

    def compute(j):
        load(j).wait()

        @pl.loop(0, 2)
        def _(half):
            cols = pl.ds(pl.multiple_of(half * 256, 256), 256)
            acc = jnp.zeros((ROWS, 256), F32)
            for b in range(N):
                acc = acc + dot_nn(normed[:, b * PIECE : b * PIECE + PIECE], wbuf[j % 2, b, :, cols])
            outs[j][:, cols] = acc.astype(BF16)

    gather.middle(0)
    for j in range(3):
        gather.middle(j + 1)
        gather.finish(j)

        @pl.when(s == 0)
        def _():
            load(j).start()
            compute(j)

    gather.close(3)


def gather_weights(wt, rows_in, gain):
    thin = jax.ShapeDtypeStruct((ROWS, PIECE), BF16)
    return pl.pallas_call(
        gather_kernel,
        name="gather_weights",
        out_shape=(
            jax.ShapeDtypeStruct((4, N, PIECE, PIECE), BF16),
            jax.ShapeDtypeStruct((ROWS, D), BF16),
            thin,
            thin,
            thin,
        ),
        in_specs=[VM, VM, VM],
        out_specs=(HBM, VM, VM, VM, VM),
        scratch_shapes=[
            pltpu.VMEM((2, N, PIECE, PIECE), BF16),
            DMA((2,)),
            DMA((4, 8)),
            DMA((4, 8)),
            DMA((4,)),
        ],
        compiler_params=pltpu.CompilerParams(collective_id=0, has_side_effects=True),
    )(wt, rows_in, gain)


class Relay:
    def __init__(self, terms, resid, total, bufs, sems):
        self.terms, self.resid = terms, resid
        (self.one, self.direct, self.passed, self.mixed, self.kept, self.cross, self.over, self.summed, self.landed) = bufs
        self.send, self.recv, g_send, g_recv, g_loc = sems
        s, d, m = coords()
        x, y = m // 4, m % 4
        self.x, self.y, self.m = x, y, m
        self.up, self.down, self.opp = (y + 1) % 4, (y + 3) % 4, (y + 2) % 4
        self.to_up, self.to_down = (s, d, x * 4 + self.up), (s, d, x * 4 + self.down)
        self.to_x = (s, d, (1 - x) * 4 + y)
        self.partner = (1 - s, d, (1 - x) * 4 + y)
        self.gather = MpGather(
            CHUNKS,
            lambda c: self.landed.at[self.rows(c)],
            lambda mm, c: piece(total, (mm + 4) % N, c * CH),
            g_send,
            g_recv,
            g_loc,
        )

    def rows(self, c):
        return pl.ds(c * CH, CH)

    def cp(self, c, kind, src, dst, to):
        return rc(src, dst, self.send.at[c, kind], self.recv.at[c, kind], to)

    def copy(self, c, kind):
        rows = self.rows(c)
        return (
            lambda: self.cp(c, 0, piece(self.terms, self.opp, c * CH), self.one.at[0, rows], self.to_up),
            lambda: self.cp(c, 1, piece(self.terms, 4 + self.opp, c * CH), self.one.at[1, rows], self.to_down),
            lambda: self.cp(c, 2, piece(self.terms, 4 + self.up, c * CH), self.direct.at[1, rows], self.to_up),
            lambda: self.cp(c, 3, piece(self.terms, self.down, c * CH), self.direct.at[0, rows], self.to_down),
            lambda: self.cp(c, 4, self.mixed.at[0, rows], self.passed.at[0, rows], self.to_up),
            lambda: self.cp(c, 5, self.mixed.at[1, rows], self.passed.at[1, rows], self.to_down),
            lambda: self.cp(c, 6, self.cross.at[rows], self.over.at[rows], self.to_x),
            lambda: self.cp(c, 7, self.summed.at[rows], self.landed.at[rows], self.partner),
        )[kind]()

    def mine(self, index, c):
        return self.terms[pl.ds(c * CH, CH), pl.ds(pl.multiple_of(index * PIECE, PIECE), PIECE)].astype(F32)

    def stage(self, c, number):
        if not 0 <= c < CHUNKS:
            return
        rows = self.rows(c)
        if number == 1:
            for side, index in ((0, self.up), (1, 4 + self.down)):
                self.copy(c, side).wait_recv()
                value = self.one[side, rows].astype(F32) + self.mine(index, c)
                self.mixed[side, rows] = value.astype(BF16)
                self.copy(c, 4 + side).start()
            for kind in (2, 3):
                self.copy(c, kind).start()
        elif number == 2:
            for kind in range(2, 6):
                self.copy(c, kind).wait_recv()
            for side in range(2):
                value = self.direct[side, rows].astype(F32) + self.passed[side, rows].astype(F32)
                value = value + self.mine(side * 4 + self.y, c)

                @pl.when(self.x == side)
                def _():
                    self.kept[rows] = value

                @pl.when(self.x != side)
                def _():
                    self.cross[rows] = value.astype(BF16)

            self.copy(c, 6).start()
        else:
            self.copy(c, 6).wait_recv()
            value = self.kept[rows] + self.over[rows].astype(F32)
            if self.with_resid:
                value = value + self.resid[rows].astype(F32)
            self.summed[rows] = value.astype(BF16)
            self.copy(c, 7).start()

    def sender_open(self):
        for c in range(CHUNKS):
            for kind in range(2):
                self.copy(c, kind).start()

    def sender(self, with_resid):
        self.with_resid = with_resid
        for tick in range(CHUNKS + 2):
            for number in range(1, 4):
                self.stage(tick + 1 - number, number)

    def sender_close(self):
        for c in range(CHUNKS):
            for kind in range(8):
                self.copy(c, kind).wait_send()

    def taker(self):
        for tick in range(CHUNKS + 3):
            if tick < CHUNKS:
                self.copy(tick, 7).wait_recv()
            for number in range(4):
                self.gather.stage(tick - number, number)


SIDES = pltpu.VMEM((2, ROWS, PIECE), BF16)
ONE = pltpu.VMEM((ROWS, PIECE), BF16)
RELAY_BUFS = [SIDES, SIDES, SIDES, SIDES, pltpu.VMEM((ROWS, PIECE), F32), ONE, ONE, ONE, ONE]
RELAY_SEMS = [DMA((CHUNKS, 8)), DMA((CHUNKS, 8)), DMA((CHUNKS, 7)), DMA((CHUNKS, 7)), DMA((CHUNKS,))]


def bridge_kernel(
    lens, q_in, k_in, v_in, rows_in, xa, cot, mats, ctx_ref, gq_ref, gk_ref, gv_ref, total, norm, rights, slices, *rest
):
    s, d, m = coords()
    greet(mp_near(s, d, m) + dp_near(s, d, m) + [(1 - s, d, (m + 4) % N)], (d != m, (s, m, d)))
    bufs, sems = rest[:9], rest[9:14]
    (y_send, y_recv, y_loc, w_sem, wbuf, terms, q_mid, k_mid, v_mid, g_mid, gram_a, gram_b) = rest[14:26]
    xb, resid, r_sem, turn, t_send, t_recv, t_loc, b_send, b_recv, b_loc = rest[26:]

    def slot(i, ref):
        return SliceGather(
            piece(ref, m),
            turn.at[i],
            slices.at[i],
            t_send.at[i],
            t_recv.at[i],
            t_loc.at[i],
            b_send.at[i],
            b_recv.at[i],
            b_loc.at[i],
        )

    slot_a, slot_b = slot(0, xa), slot(1, xb)
    relay = Relay(terms, resid, total, bufs, sems)
    gather = DpGather(
        1,
        lambda j: ctx_ref,
        lambda j, b: rights.at[3, pl.ds(pl.multiple_of(b * ROWS, ROWS), ROWS)],
        lambda j, b, h: rights.at[3, pl.ds(pl.multiple_of(b * ROWS + h * 128, 128), 128)],
        y_send,
        y_recv,
        y_loc,
    )

    def load(mat, slot):
        return pltpu.make_async_copy(mats.at[mat], wbuf.at[slot], w_sem.at[slot])

    def block(slot, index):
        return wbuf[slot, pl.ds(pl.multiple_of(index * PIECE, PIECE), PIECE)]

    def put(index, value):
        terms[:, pl.ds(pl.multiple_of(index * PIECE, PIECE), PIECE)] = value.astype(BF16)

    def send_terms(term):
        for group in ((relay.opp, 4 + relay.opp), (relay.up, 4 + relay.down, 4 + relay.up, relay.down)):
            for index in group:
                put(index, term(index))
            if group[0] is relay.opp:
                relay.sender_open()
        for index in (relay.y, 4 + relay.y):
            put(index, term(index))

    def grams(src, dst):
        for e in range(2):
            rows = src[pl.ds(e * 128, 128)]
            dst[e] = dot_nt(rows, rows)

    def thin_gram(ref, e):
        rows = ref[pl.ds(e * 128, 128)]
        return dot_nt(rows, rows)

    def note(value_of):
        lane = lax.broadcasted_iota(jnp.int32, (8, 128), 1)
        norm[...] = jnp.where(lane == 0, jnp.sum(value_of(0)), 0.0) + jnp.where(lane == 1, jnp.sum(value_of(1)), 0.0)

    def wide_dot(left, slot, out):
        for half in range(2):
            cols = slice(half * 256, half * 256 + 256)
            out[:, cols] = dot_nn(left[...], wbuf[slot, :, cols]).astype(BF16)

    def each_head(body):
        @pl.loop(0, 2)
        def _(e):
            rows = pl.ds(pl.multiple_of(e * 128, 128), 128)
            key_ok = lax.broadcasted_iota(jnp.int32, (128, 128), 1) < lens[0, e]
            for pair in range(4):
                body(rows, slice(pair * 128, pair * 128 + 128), key_ok)

    @pl.when(s == 0)
    def _():
        load(3, 0).start()
        bring = pltpu.make_async_copy(piece(rows_in, m), resid, r_sem)
        bring.start()

        def ahead(rows, cols, key_ok):
            ctx_ref[rows, cols] = context(q_in[rows, cols], k_in[rows, cols], v_in[rows, cols], key_ok)

        each_head(ahead)
        gather.open()
        load(3, 0).wait()
        bring.wait()
        send_terms(lambda index: dot_nt(ctx_ref[...], block(0, index)))
        relay.sender(True)
        slot_a.open()
        gather.middle(0)
        slot_a.middle()
        grams(xa, gram_a)
        slot_a.second()
        gather.close()
        slot_a.third()
        slot_a.close()
        relay.taker()
        wide_dot(total, 0, g_mid)

        def back(rows, cols, key_ok):
            _, gq, gk, gv = gradients(
                q_in[rows, cols], k_in[rows, cols], v_in[rows, cols], g_mid[rows, cols], key_ok, False
            )
            gq_ref[rows, cols], gk_ref[rows, cols], gv_ref[rows, cols] = gq, gk, gv

        each_head(back)
        grams(total, gram_b)
        note(
            lambda e: gram_a[e] * (thin_gram(gq_ref, e) + thin_gram(gk_ref, e) + thin_gram(gv_ref, e))
            + gram_b[e] * thin_gram(ctx_ref, e)
        )
        relay.sender_close()
        relay.gather.close()

    @pl.when(s == 1)
    def _():
        load(0, 0).start()
        load(3, 1).start()
        slot_a.open()

        @pl.loop(0, ROWS // 32)
        def _(i):
            rows = pl.ds(pl.multiple_of(i * 32, 32), 32)
            place = lax.rem(i, 4) * 32 + lax.broadcasted_iota(jnp.int32, (32, D), 0)
            value = cot[rows]
            xb[rows] = jnp.where(place < lens[1, i // 4], value, jnp.zeros_like(value))

        slot_a.middle()
        load(0, 0).wait()
        load(3, 1).wait()
        wide_dot(xa, 0, q_mid)
        slot_a.second()
        wide_dot(xb, 1, g_mid)
        slot_a.third()
        load(1, 0).start()
        load(2, 1).start()
        grams(xa, gram_a)
        grams(xb, gram_b)
        slot_a.close()
        load(1, 0).wait()
        load(2, 1).wait()
        relay.taker()
        wide_dot(total, 0, k_mid)
        wide_dot(total, 1, v_mid)

        def both(rows, cols, key_ok):
            ctx, gq, gk, gv = gradients(
                q_mid[rows, cols], k_mid[rows, cols], v_mid[rows, cols], g_mid[rows, cols], key_ok, True
            )
            ctx_ref[rows, cols], gq_ref[rows, cols], gk_ref[rows, cols], gv_ref[rows, cols] = ctx, gq, gk, gv

        each_head(both)
        send_terms(lambda index: dot_nt(gk_ref[...], block(0, index)) + dot_nt(gv_ref[...], block(1, index)))
        gather.open()
        relay.sender(False)
        slot_b.open()
        gather.middle(0)
        slot_b.middle()

        def value_of(e):
            rows = total[pl.ds(e * 128, 128)]
            return (
                gram_a[e] * thin_gram(gq_ref, e)
                + dot_nt(rows, rows) * (thin_gram(gk_ref, e) + thin_gram(gv_ref, e))
                + gram_b[e] * thin_gram(ctx_ref, e)
            )

        note(value_of)
        slot_b.second()
        gather.close()
        slot_b.third()
        slot_b.close()
        relay.sender_close()
        relay.gather.close()


def bridge(lens, q, k, v, rows_in, xa, cot, mats):
    thin = jax.ShapeDtypeStruct((ROWS, PIECE), BF16)
    small = pltpu.VMEM((ROWS, PIECE), BF16)
    square = pltpu.VMEM((2, 128, 128), F32)
    return pl.pallas_call(
        bridge_kernel,
        name="bridge",
        out_shape=(thin,) * 4
        + (
            jax.ShapeDtypeStruct((ROWS, D), BF16),
            jax.ShapeDtypeStruct((8, 128), F32),
            jax.ShapeDtypeStruct((4, N * ROWS, PIECE), BF16),
            jax.ShapeDtypeStruct((3, N * ROWS, PIECE), BF16),
        ),
        in_specs=[SM] + [VM] * 3 + [HBM, VM, VM, HBM],
        out_specs=(VM,) * 6 + (HBM, HBM),
        scratch_shapes=RELAY_BUFS
        + RELAY_SEMS
        + [
            DMA((1, 8)),
            DMA((1, 8)),
            DMA((1,)),
            DMA((2,)),
            pltpu.VMEM((2, D, PIECE), BF16),
            pltpu.VMEM((ROWS, D), BF16),
            small,
            small,
            small,
            small,
            square,
            square,
            pltpu.VMEM((ROWS, D), BF16),
            small,
            DMA,
            pltpu.VMEM((2, ROWS, PIECE), BF16),
            DMA((2,)),
            DMA((2,)),
            DMA((2,)),
            DMA((2, SLICE_CHUNKS, 7)),
            DMA((2, SLICE_CHUNKS, 7)),
            DMA((2, SLICE_CHUNKS)),
        ],
        compiler_params=pltpu.CompilerParams(collective_id=1, has_side_effects=True),
    )(lens, q, k, v, rows_in, xa, cot, mats)


def final_kernel(
    gq, gk, gv, relayed, norm, slices_in, rights_in, slices, rights, norms,
    turn, norm_mp, norm_own, norm_far, norm_dp,
    y_send, y_recv, y_loc, t_send, t_recv, t_loc, b_send, b_recv, b_loc, n_send, n_recv, f_send, f_recv, e_send, e_recv,
):
    s, d, m = coords()
    dp_all = [(s, (d + i) % N, m) for i in range(1, N)]
    greet(mp_peers(s, d, m) + dp_all + [(1 - s, d, m)], (d != m, (s, m, d)))
    parts = (gq, gk, gv)
    gather = DpGather(
        3,
        lambda j: parts[j],
        lambda j, b: rights.at[j, pl.ds(pl.multiple_of(b * ROWS, ROWS), ROWS)],
        lambda j, b, h: rights.at[j, pl.ds(pl.multiple_of(b * ROWS + h * 128, 128), 128)],
        y_send,
        y_recv,
        y_loc,
    )
    slot = SliceGather(
        piece(relayed, m), turn, slices.at[2], t_send, t_recv, t_loc, b_send, b_recv, b_loc
    )

    def to_mp(i):
        return rc(norm, norm_mp.at[m], n_send.at[i - 1], n_recv.at[i - 1], (s, d, (m + i) % N))

    def from_mp(i):
        ref = norm_mp.at[(m + N - i) % N]
        return rc(ref, ref, n_send.at[i - 1], n_recv.at[i - 1], (s, d, (m + i) % N))

    def to_dp(i):
        return rc(norm_dp, norms.at[d], e_send.at[i - 1], e_recv.at[i - 1], (s, (d + i) % N, m))

    def from_dp(i):
        ref = norms.at[(d + N - i) % N]
        return rc(ref, ref, e_send.at[i - 1], e_recv.at[i - 1], (s, (d + i) % N, m))

    slot.open()
    for i in range(1, N):
        to_mp(i).start()
    gather.open()
    norm_mp[m] = norm[...]
    for i in range(1, N):
        from_mp(i).wait_recv()
    acc = norm_mp[0]
    for i in range(1, N):
        acc = acc + norm_mp[i]
    norm_own[...] = acc
    over = rc(norm_own, norm_far, f_send, f_recv, (1 - s, d, m))
    over.start()
    slot.middle()
    gather.middle(0)
    slot.second()
    over.wait_recv()
    both = norm_own[...] + norm_far[...]
    norm_dp[...] = both
    norms[d] = both
    for i in range(1, N):
        to_dp(i).start()
    slot.third()
    gather.middle(1)
    gather.middle(2)
    gather.close()
    slot.close()
    for i in range(1, N):
        from_dp(i).wait_recv()
    for i in range(1, N):
        to_mp(i).wait_send()
        to_dp(i).wait_send()
    over.wait_send()


def gather_grads(gq, gk, gv, relayed, norm, slices, rights):
    small = pltpu.VMEM((8, 128), F32)
    return pl.pallas_call(
        final_kernel,
        name="gather_grads",
        out_shape=(
            jax.ShapeDtypeStruct(slices.shape, BF16),
            jax.ShapeDtypeStruct(rights.shape, BF16),
            jax.ShapeDtypeStruct((N, 8, 128), F32),
        ),
        in_specs=[VM, VM, VM, ANY, VM, HBM, HBM],
        out_specs=(HBM, HBM, VM),
        scratch_shapes=[
            pltpu.VMEM((ROWS, PIECE), BF16),
            pltpu.VMEM((N, 8, 128), F32),
            small,
            small,
            small,
            DMA((3, 8)),
            DMA((3, 8)),
            DMA((3,)),
            DMA,
            DMA,
            DMA,
            DMA((SLICE_CHUNKS, 7)),
            DMA((SLICE_CHUNKS, 7)),
            DMA((SLICE_CHUNKS,)),
            DMA((7,)),
            DMA((7,)),
            DMA,
            DMA,
            DMA((7,)),
            DMA((7,)),
        ],
        input_output_aliases={5: 0, 6: 1},
        compiler_params=pltpu.CompilerParams(collective_id=3, has_side_effects=True),
    )(gq, gk, gv, relayed, norm, slices, rights)


def dot_nt(a, b):
    return lax.dot_general(a, b, (((1,), (1,)), ((), ())), preferred_element_type=F32)


def dot_nn(a, b):
    return lax.dot_general(a, b, (((1,), (0,)), ((), ())), preferred_element_type=F32)


def dot_tn(a, b):
    return lax.dot_general(a, b, (((0,), (0,)), ((), ())), preferred_element_type=F32)


def head_masks():
    lane = lax.broadcasted_iota(jnp.int32, (128, 128), 1)
    return lane < HEAD, lane >= HEAD


def soft(q, k, mask, key_ok):
    zero = jnp.zeros_like(q)
    scores = dot_nt(jnp.where(mask, q, zero), k) * HEAD ** (-0.5)
    scores = jnp.where(key_ok, scores, -jnp.inf)
    weights = jnp.exp(scores - jnp.max(scores, axis=-1, keepdims=True))
    return weights / jnp.sum(weights, axis=-1, keepdims=True)


def context(q, k, v, key_ok):
    zero = jnp.zeros_like(q)
    ctx = jnp.zeros((128, 128), F32)
    for mask in head_masks():
        probs = soft(q, k, mask, key_ok)
        ctx = ctx + dot_nn(probs.astype(BF16), jnp.where(mask, v, zero))
    return ctx.astype(BF16)


def gradients(q, k, v, g, key_ok, with_context):
    zero = jnp.zeros_like(q)
    ctx = gq = gk = gv = jnp.zeros((128, 128), F32)
    for mask in head_masks():
        probs = soft(q, k, mask, key_ok)
        low = probs.astype(BF16)
        g_one = jnp.where(mask, g, zero)
        gp = dot_nt(g_one, v)
        inner = jnp.sum(gp * probs, axis=-1, keepdims=True)
        gs = (probs * (gp - inner) * HEAD ** (-0.5)).astype(BF16)
        if with_context:
            ctx = ctx + dot_nn(low, jnp.where(mask, v, zero))
        gq = gq + dot_nn(gs, jnp.where(mask, k, zero))
        gk = gk + dot_tn(gs, jnp.where(mask, q, zero))
        gv = gv + dot_tn(low, g_one)
    return tuple(value.astype(BF16) for value in (ctx, gq, gk, gv))


BLOCK = 128


def weight_kernel(sec, clip, x_ref, y_ref, noise_ref, out_ref, scaled):
    @pl.when(pl.program_id(0) == 0)
    def _():
        for mat in range(4):

            @pl.loop(0, 16)
            def _(e):
                rows = pl.ds(pl.multiple_of(e * 128, 128), 128)
                scaled[mat, rows] = (y_ref[mat, rows].astype(F32) * clip[e]).astype(BF16)

    is_dec = sec[0]
    picks = (0, 2 * is_dec, 2 * is_dec, 2 - is_dec)
    for mat in range(4):
        total = dot_tn(x_ref[picks[mat]], scaled[mat])
        out_ref[:, mat, :] = (total + noise_ref[:, mat, :]) * (1.0 / 16.0)


def weight_grads(sec, clip, slices, rights, dp_noise):
    wide = pl.BlockSpec((BLOCK, 4, PIECE), lambda b: (b, 0, 0))
    return pl.pallas_call(
        weight_kernel,
        name="weight_grads",
        grid=(PIECE // BLOCK,),
        in_specs=[
            SM,
            SM,
            pl.BlockSpec((3, N * ROWS, BLOCK), lambda b: (0, 0, b)),
            pl.BlockSpec((4, N * ROWS, PIECE), lambda b: (0, 0, 0), pipeline_mode=pl.Buffered(1)),
            wide,
        ],
        out_specs=wide,
        out_shape=jax.ShapeDtypeStruct((PIECE, 4, PIECE), F32),
        scratch_shapes=[pltpu.VMEM((4, N * ROWS, PIECE), BF16)],
    )(sec, clip, slices, rights, dp_noise)


def per_device(inputs, norm_gains, weights, cotangent, lengths, dp_noise):
    sec = jnp.reshape(lax.axis_index("section"), (1,)).astype(jnp.int32)
    rows_in = inputs[0].reshape(ROWS, D)
    wt = jnp.swapaxes(weights[0], 0, 1)
    full, normed, q, k, v = gather_weights(wt, rows_in, norm_gains)
    mats = full.reshape(4, D, PIECE)
    ctx, gq, gk, gv, relayed, norm, rights, slices = bridge(
        lengths, q, k, v, rows_in, normed, cotangent.reshape(ROWS, D), mats
    )
    slices, rights, norms = gather_grads(gq, gk, gv, relayed, norm, slices, rights)
    sq_norm = norms[:, 0, :2]
    bound = jnp.sqrt(jnp.float32(8.0 * D * HEADS * HEAD))
    clip_all = bound / (jnp.sqrt(sq_norm) + 0.01 * bound)
    clip_scale = lax.dynamic_index_in_dim(clip_all, lax.axis_index("dp"), 0, keepdims=False)
    noisy_grad = weight_grads(sec, clip_all.reshape(16), slices, rights, dp_noise[0])
    return (noisy_grad[None], clip_scale)


def solution(mesh):
    placed = (
        P("section", "dp", None, None),
        P("section", None),
        P("section", "dp", None, "mp"),
        P("dp", None, None),
        P(None, "dp"),
        P("section", "dp", None, "mp"),
    )
    return jax.shard_map(
        per_device,
        mesh=mesh,
        in_specs=placed,
        out_specs=(P("section", "dp", None, "mp"), P("dp")),
        check_vma=False,
    )
```

```python
import functools

import jax
import jax.numpy as jnp
from jax import lax
from jax.experimental import pallas as pl
from jax.experimental.pallas import tpu as pltpu
from jax.sharding import PartitionSpec as P

D = 4096
HEADS = 64
HEAD = 64
MESH = pl.DeviceIdType.MESH
F32 = jnp.float32
BF16 = jnp.bfloat16
N = 8
ROWS = 256
PIECE = 512
CHUNKS = 4
CH = ROWS // CHUNKS
ANY = pl.BlockSpec(memory_space=pl.ANY)
HBM = pl.BlockSpec(memory_space=pltpu.HBM)
VM = pl.BlockSpec(memory_space=pltpu.VMEM)
SM = pl.BlockSpec(memory_space=pltpu.SMEM)
DMA = pltpu.SemaphoreType.DMA


def rc(src, dst, send_sem, recv_sem, dev):
    return pltpu.make_async_remote_copy(
        src_ref=src,
        dst_ref=dst,
        send_sem=send_sem,
        recv_sem=recv_sem,
        device_id=dev,
        device_id_type=MESH,
    )


def coords():
    return lax.axis_index("section"), lax.axis_index("dp"), lax.axis_index("mp")


def greet(devs, extra=None):
    barrier = pltpu.get_barrier_semaphore()
    for dev in devs:
        pl.semaphore_signal(barrier, inc=1, device_id=dev, device_id_type=MESH)
    if extra is not None:
        cond, dev = extra

        @pl.when(cond)
        def _():
            pl.semaphore_signal(barrier, inc=1, device_id=dev, device_id_type=MESH)

        pl.semaphore_wait(barrier, len(devs) + jnp.where(cond, 1, 0))
    else:
        pl.semaphore_wait(barrier, len(devs))


def mp_peers(s, d, m):
    return [(s, d, (m + i) % N) for i in range(1, N)]


def dp_near(s, d, m):
    return [(s, (d + 2) % N, m), (s, (d + 6) % N, m), (s, d + 1 - 2 * (d % 2), m)]


class DpGather:
    def __init__(self, count, own, dst, half, send, recv, local):
        self.n, self.own, self.dst, self.half = count, own, dst, half
        self.send, self.recv, self.local = send, recv, local
        s, d, m = coords()
        self.d = d
        self.left, self.right, self.far = (d + 6) % N, (d + 2) % N, (d + 4) % N
        self.sib = d + 1 - 2 * (d % 2)
        self.to_right, self.to_left = (s, self.right, m), (s, self.left, m)
        self.to_sib = (s, self.sib, m)

    def cp(self, j, kind, src, dst, dev):
        return rc(src, dst, self.send.at[j, kind], self.recv.at[j, kind], dev)

    def keep(self, j):
        return pltpu.make_async_copy(self.own(j), self.dst(j, self.d), self.local.at[j])

    def out(self, j, kind):
        d = self.d
        if kind == 0:
            return self.cp(j, 0, self.own(j), self.dst(j, d), self.to_right)
        if kind == 1:
            return self.cp(j, 1, self.own(j), self.dst(j, d), self.to_left)
        if kind == 2:
            ref = self.half(j, self.left, 0)
            return self.cp(j, 2, ref, ref, self.to_right)
        if kind == 3:
            ref = self.half(j, self.right, 1)
            return self.cp(j, 3, ref, ref, self.to_left)
        if kind == 4:
            return self.cp(j, 4, self.own(j), self.dst(j, d), self.to_sib)
        block = (self.left, self.right, self.far)[kind - 5]
        return self.cp(j, kind, self.dst(j, block), self.dst(j, block), self.to_sib)

    def into(self, j, kind):
        sib = self.sib
        if kind == 0:
            ref = self.dst(j, self.left)
        elif kind == 1:
            ref = self.dst(j, self.right)
        elif kind == 2:
            ref = self.half(j, self.far, 0)
        elif kind == 3:
            ref = self.half(j, self.far, 1)
        else:
            ref = self.dst(j, (sib, (sib + 6) % N, (sib + 2) % N, (sib + 4) % N)[kind - 4])
        return self.cp(j, kind, ref, ref, self.to_sib)

    def begin(self, j):
        self.out(j, 0).start()
        self.out(j, 1).start()
        self.out(j, 4).start()
        self.keep(j).start()

    def open(self):
        for j in range(min(2, self.n)):
            self.begin(j)

    def far_on(self, j):
        self.into(j, 2).wait_recv()
        self.into(j, 3).wait_recv()
        self.out(j, 7).start()

    def middle(self, j):
        self.into(j, 0).wait_recv()
        self.into(j, 1).wait_recv()
        self.out(j, 2).start()
        self.out(j, 3).start()
        self.out(j, 5).start()
        self.out(j, 6).start()
        if j + 2 < self.n:
            self.begin(j + 2)
        if j > 0:
            self.far_on(j - 1)

    def finish(self, j):
        for kind in range(4, 8):
            self.into(j, kind).wait_recv()
        self.keep(j).wait()

    def close(self, finished=0):
        self.far_on(self.n - 1)
        for j in range(finished, self.n):
            self.finish(j)
        for j in range(self.n):
            for kind in range(8):
                self.out(j, kind).wait_send()


class MpGather:
    def __init__(self, chunks, source, slot, send, recv, local):
        s, d, m = coords()
        self.chunks, self.source, self.slot = chunks, source, slot
        self.send, self.recv, self.local = send, recv, local
        x, y = m // 4, m % 4
        up, down, far = (y + 1) % 4, (y + 3) % 4, (y + 2) % 4
        self.m, self.xm = m, (1 - x) * 4 + y
        self.to = ((s, d, self.xm), (s, d, x * 4 + up), (s, d, x * 4 + down))
        self.sources = (m, m, m, self.xm, self.xm, down, 4 + up)
        self.landing = (
            self.xm,
            x * 4 + down,
            x * 4 + up,
            (1 - x) * 4 + down,
            (1 - x) * 4 + up,
            far,
            4 + far,
        )

    def out(self, c, kind):
        dest = self.slot(self.sources[kind], c)
        src = self.source(c) if kind < 3 else dest
        to = self.to[(0, 1, 2, 1, 2, 1, 2)[kind]]
        return rc(src, dest, self.send.at[c, kind], self.recv.at[c, kind], to)

    def into(self, c, kind):
        ref = self.slot(self.landing[kind], c)
        return rc(ref, ref, self.send.at[c, kind], self.recv.at[c, kind], self.to[0])

    def keep(self, c):
        return pltpu.make_async_copy(self.source(c), self.slot(self.m, c), self.local.at[c])

    def stage(self, c, number):
        if not 0 <= c < self.chunks:
            return
        waits, starts = (((), (0, 1, 2)), ((0,), (3, 4)), ((1, 2, 3, 4), (5, 6)), ((5, 6), ()))[number]
        for kind in waits:
            self.into(c, kind).wait_recv()
        for kind in starts:
            self.out(c, kind).start()
        if number == 0:
            self.keep(c).start()
        if number == 3:
            self.keep(c).wait()

    def close(self):
        for c in range(self.chunks):
            for kind in range(7):
                self.out(c, kind).wait_send()


def mp_near(s, d, m):
    x, y = m // 4, m % 4
    return [(s, d, (1 - x) * 4 + y), (s, d, x * 4 + (y + 1) % 4), (s, d, x * 4 + (y + 3) % 4)]


SLICE_CHUNKS = 2


class SliceGather:
    def __init__(self, source, turn, dest, send_t, recv_t, local_t, send, recv, local):
        s, d, m = coords()
        self.d, self.m = d, m
        self.far = lambda: rc(source, turn, send_t, recv_t, (s, m, d))
        self.near = lambda: pltpu.make_async_copy(source, turn, local_t)
        step = ROWS // SLICE_CHUNKS
        self.gather = MpGather(
            SLICE_CHUNKS,
            lambda c: turn.at[pl.ds(c * step, step)],
            lambda mm, c: dest.at[pl.ds(pl.multiple_of(mm * ROWS + c * step, step), step)],
            send,
            recv,
            local,
        )

    def open(self):
        pl.when(self.d != self.m)(lambda: self.far().start())
        pl.when(self.d == self.m)(lambda: self.near().start())

    def middle(self):
        pl.when(self.d != self.m)(lambda: self.far().wait_recv())
        pl.when(self.d == self.m)(lambda: self.near().wait())
        for c in range(SLICE_CHUNKS):
            self.gather.stage(c, 0)

    def second(self):
        for c in range(SLICE_CHUNKS):
            self.gather.stage(c, 1)

    def third(self):
        for c in range(SLICE_CHUNKS):
            self.gather.stage(c, 2)

    def close(self):
        for c in range(SLICE_CHUNKS):
            self.gather.stage(c, 3)
        self.gather.close()
        pl.when(self.d != self.m)(lambda: self.far().wait_send())


def piece(ref, m, rows=None):
    cols = pl.ds(pl.multiple_of(m * PIECE, PIECE), PIECE)
    if rows is None:
        return ref.at[:, cols]
    return ref.at[pl.ds(rows, CH), cols]


def gather_kernel(wt, rows_in, gain, full, normed, q_ref, k_ref, v_ref, wbuf, w_sem, w_send, w_recv, w_loc):
    s, d, m = coords()
    greet(dp_near(s, d, m))
    gather = DpGather(
        4,
        lambda j: wt.at[j],
        lambda j, b: full.at[j, b],
        lambda j, b, h: full.at[j, b, pl.ds(h * 256, 256)],
        w_send,
        w_recv,
        w_loc,
    )
    gather.open()

    @pl.loop(0, ROWS // 32)
    def _(i):
        rows = pl.ds(pl.multiple_of(i * 32, 32), 32)
        value = rows_in[rows].astype(F32)
        inverse = lax.rsqrt(jnp.mean(value * value, axis=-1, keepdims=True) + 1e-06)
        normed[rows] = (value * inverse * gain[...].astype(F32)).astype(BF16)

    outs = (q_ref, k_ref, v_ref)

    def load(j):
        return pltpu.make_async_copy(full.at[j], wbuf.at[j % 2], w_sem.at[j % 2])

    def compute(j):
        load(j).wait()

        @pl.loop(0, 2)
        def _(half):
            cols = pl.ds(pl.multiple_of(half * 256, 256), 256)
            acc = jnp.zeros((ROWS, 256), F32)
            for b in range(N):
                acc = acc + dot_nn(normed[:, b * PIECE : b * PIECE + PIECE], wbuf[j % 2, b, :, cols])
            outs[j][:, cols] = acc.astype(BF16)

    gather.middle(0)
    for j in range(3):
        gather.middle(j + 1)
        gather.finish(j)

        @pl.when(s == 0)
        def _():
            load(j).start()
            compute(j)

    gather.close(3)


def gather_weights(wt, rows_in, gain):
    thin = jax.ShapeDtypeStruct((ROWS, PIECE), BF16)
    return pl.pallas_call(
        gather_kernel,
        name="gather_weights",
        out_shape=(
            jax.ShapeDtypeStruct((4, N, PIECE, PIECE), BF16),
            jax.ShapeDtypeStruct((ROWS, D), BF16),
            thin,
            thin,
            thin,
        ),
        in_specs=[VM, VM, VM],
        out_specs=(HBM, VM, VM, VM, VM),
        scratch_shapes=[
            pltpu.VMEM((2, N, PIECE, PIECE), BF16),
            DMA((2,)),
            DMA((4, 8)),
            DMA((4, 8)),
            DMA((4,)),
        ],
        compiler_params=pltpu.CompilerParams(collective_id=0, has_side_effects=True),
    )(wt, rows_in, gain)


class Relay:
    def __init__(self, terms, resid, total, bufs, sems):
        self.terms, self.resid = terms, resid
        (self.one, self.direct, self.passed, self.mixed, self.kept, self.cross, self.over, self.summed, self.landed) = bufs
        self.send, self.recv, g_send, g_recv, g_loc = sems
        s, d, m = coords()
        x, y = m // 4, m % 4
        self.x, self.y, self.m = x, y, m
        self.up, self.down, self.opp = (y + 1) % 4, (y + 3) % 4, (y + 2) % 4
        self.to_up, self.to_down = (s, d, x * 4 + self.up), (s, d, x * 4 + self.down)
        self.to_x = (s, d, (1 - x) * 4 + y)
        self.partner = (1 - s, d, (1 - x) * 4 + y)
        self.gather = MpGather(
            CHUNKS,
            lambda c: self.landed.at[self.rows(c)],
            lambda mm, c: piece(total, (mm + 4) % N, c * CH),
            g_send,
            g_recv,
            g_loc,
        )

    def rows(self, c):
        return pl.ds(c * CH, CH)

    def cp(self, c, kind, src, dst, to):
        return rc(src, dst, self.send.at[c, kind], self.recv.at[c, kind], to)

    def copy(self, c, kind):
        rows = self.rows(c)
        return (
            lambda: self.cp(c, 0, piece(self.terms, self.opp, c * CH), self.one.at[0, rows], self.to_up),
            lambda: self.cp(c, 1, piece(self.terms, 4 + self.opp, c * CH), self.one.at[1, rows], self.to_down),
            lambda: self.cp(c, 2, piece(self.terms, 4 + self.up, c * CH), self.direct.at[1, rows], self.to_up),
            lambda: self.cp(c, 3, piece(self.terms, self.down, c * CH), self.direct.at[0, rows], self.to_down),
            lambda: self.cp(c, 4, self.mixed.at[0, rows], self.passed.at[0, rows], self.to_up),
            lambda: self.cp(c, 5, self.mixed.at[1, rows], self.passed.at[1, rows], self.to_down),
            lambda: self.cp(c, 6, self.cross.at[rows], self.over.at[rows], self.to_x),
            lambda: self.cp(c, 7, self.summed.at[rows], self.landed.at[rows], self.partner),
        )[kind]()

    def mine(self, index, c):
        return self.terms[pl.ds(c * CH, CH), pl.ds(pl.multiple_of(index * PIECE, PIECE), PIECE)].astype(F32)

    def stage(self, c, number):
        if not 0 <= c < CHUNKS:
            return
        rows = self.rows(c)
        if number == 1:
            for side, index in ((0, self.up), (1, 4 + self.down)):
                self.copy(c, side).wait_recv()
                value = self.one[side, rows].astype(F32) + self.mine(index, c)
                self.mixed[side, rows] = value.astype(BF16)
                self.copy(c, 4 + side).start()
            for kind in (2, 3):
                self.copy(c, kind).start()
        elif number == 2:
            for kind in range(2, 6):
                self.copy(c, kind).wait_recv()
            for side in range(2):
                value = self.direct[side, rows].astype(F32) + self.passed[side, rows].astype(F32)
                value = value + self.mine(side * 4 + self.y, c)

                @pl.when(self.x == side)
                def _():
                    self.kept[rows] = value

                @pl.when(self.x != side)
                def _():
                    self.cross[rows] = value.astype(BF16)

            self.copy(c, 6).start()
        else:
            self.copy(c, 6).wait_recv()
            value = self.kept[rows] + self.over[rows].astype(F32)
            if self.with_resid:
                value = value + self.resid[rows].astype(F32)
            self.summed[rows] = value.astype(BF16)
            self.copy(c, 7).start()

    def sender_open(self):
        for c in range(CHUNKS):
            for kind in range(2):
                self.copy(c, kind).start()

    def sender(self, with_resid):
        self.with_resid = with_resid
        for tick in range(CHUNKS + 2):
            for number in range(1, 4):
                self.stage(tick + 1 - number, number)

    def sender_close(self):
        for c in range(CHUNKS):
            for kind in range(8):
                self.copy(c, kind).wait_send()

    def taker(self):
        for tick in range(CHUNKS + 3):
            if tick < CHUNKS:
                self.copy(tick, 7).wait_recv()
            for number in range(4):
                self.gather.stage(tick - number, number)


SIDES = pltpu.VMEM((2, ROWS, PIECE), BF16)
ONE = pltpu.VMEM((ROWS, PIECE), BF16)
RELAY_BUFS = [SIDES, SIDES, SIDES, SIDES, pltpu.VMEM((ROWS, PIECE), F32), ONE, ONE, ONE, ONE]
RELAY_SEMS = [DMA((CHUNKS, 8)), DMA((CHUNKS, 8)), DMA((CHUNKS, 7)), DMA((CHUNKS, 7)), DMA((CHUNKS,))]


def bridge_kernel(
    lens, q_in, k_in, v_in, rows_in, xa, cot, mats, ctx_ref, gq_ref, gk_ref, gv_ref, total, norm, rights, slices, *rest
):
    s, d, m = coords()
    greet(mp_near(s, d, m) + dp_near(s, d, m) + [(1 - s, d, (m + 4) % N)], (d != m, (s, m, d)))
    bufs, sems = rest[:9], rest[9:14]
    (y_send, y_recv, y_loc, w_sem, wbuf, terms, q_mid, k_mid, v_mid, g_mid, gram_a, gram_b) = rest[14:26]
    xb, resid, r_sem, turn, t_send, t_recv, t_loc, b_send, b_recv, b_loc = rest[26:]

    def slot(i, ref):
        return SliceGather(
            piece(ref, m),
            turn.at[i],
            slices.at[i],
            t_send.at[i],
            t_recv.at[i],
            t_loc.at[i],
            b_send.at[i],
            b_recv.at[i],
            b_loc.at[i],
        )

    slot_a, slot_b = slot(0, xa), slot(1, xb)
    relay = Relay(terms, resid, total, bufs, sems)
    gather = DpGather(
        1,
        lambda j: ctx_ref,
        lambda j, b: rights.at[3, pl.ds(pl.multiple_of(b * ROWS, ROWS), ROWS)],
        lambda j, b, h: rights.at[3, pl.ds(pl.multiple_of(b * ROWS + h * 128, 128), 128)],
        y_send,
        y_recv,
        y_loc,
    )

    def load(mat, slot):
        return pltpu.make_async_copy(mats.at[mat], wbuf.at[slot], w_sem.at[slot])

    def block(slot, index):
        return wbuf[slot, pl.ds(pl.multiple_of(index * PIECE, PIECE), PIECE)]

    def put(index, value):
        terms[:, pl.ds(pl.multiple_of(index * PIECE, PIECE), PIECE)] = value.astype(BF16)

    def send_terms(term):
        for group in ((relay.opp, 4 + relay.opp), (relay.up, 4 + relay.down, 4 + relay.up, relay.down)):
            for index in group:
                put(index, term(index))
            if group[0] is relay.opp:
                relay.sender_open()
        for index in (relay.y, 4 + relay.y):
            put(index, term(index))

    def grams(src, dst):
        for e in range(2):
            rows = src[pl.ds(e * 128, 128)]
            dst[e] = dot_nt(rows, rows)

    def thin_gram(ref, e):
        rows = ref[pl.ds(e * 128, 128)]
        return dot_nt(rows, rows)

    def note(value_of):
        lane = lax.broadcasted_iota(jnp.int32, (8, 128), 1)
        norm[...] = jnp.where(lane == 0, jnp.sum(value_of(0)), 0.0) + jnp.where(lane == 1, jnp.sum(value_of(1)), 0.0)

    def wide_dot(left, slot, out):
        for half in range(2):
            cols = slice(half * 256, half * 256 + 256)
            out[:, cols] = dot_nn(left[...], wbuf[slot, :, cols]).astype(BF16)

    def each_head(body):
        @pl.loop(0, 2)
        def _(e):
            rows = pl.ds(pl.multiple_of(e * 128, 128), 128)
            key_ok = lax.broadcasted_iota(jnp.int32, (128, 128), 1) < lens[0, e]
            for pair in range(4):
                body(rows, slice(pair * 128, pair * 128 + 128), key_ok)

    @pl.when(s == 0)
    def _():
        load(3, 0).start()
        bring = pltpu.make_async_copy(piece(rows_in, m), resid, r_sem)
        bring.start()

        def ahead(rows, cols, key_ok):
            ctx_ref[rows, cols] = context(q_in[rows, cols], k_in[rows, cols], v_in[rows, cols], key_ok)

        each_head(ahead)
        gather.open()
        load(3, 0).wait()
        bring.wait()
        send_terms(lambda index: dot_nt(ctx_ref[...], block(0, index)))
        relay.sender(True)
        slot_a.open()
        gather.middle(0)
        slot_a.middle()
        grams(xa, gram_a)
        slot_a.second()
        gather.close()
        slot_a.third()
        slot_a.close()
        relay.taker()
        wide_dot(total, 0, g_mid)

        def back(rows, cols, key_ok):
            _, gq, gk, gv = gradients(
                q_in[rows, cols], k_in[rows, cols], v_in[rows, cols], g_mid[rows, cols], key_ok, False
            )
            gq_ref[rows, cols], gk_ref[rows, cols], gv_ref[rows, cols] = gq, gk, gv

        each_head(back)
        grams(total, gram_b)
        note(
            lambda e: gram_a[e] * (thin_gram(gq_ref, e) + thin_gram(gk_ref, e) + thin_gram(gv_ref, e))
            + gram_b[e] * thin_gram(ctx_ref, e)
        )
        relay.sender_close()
        relay.gather.close()

    @pl.when(s == 1)
    def _():
        load(0, 0).start()
        load(3, 1).start()
        slot_a.open()

        @pl.loop(0, ROWS // 32)
        def _(i):
            rows = pl.ds(pl.multiple_of(i * 32, 32), 32)
            place = lax.rem(i, 4) * 32 + lax.broadcasted_iota(jnp.int32, (32, D), 0)
            value = cot[rows]
            xb[rows] = jnp.where(place < lens[1, i // 4], value, jnp.zeros_like(value))

        slot_b.open()
        slot_a.middle()
        load(0, 0).wait()
        load(3, 1).wait()
        wide_dot(xa, 0, q_mid)
        slot_a.second()
        wide_dot(xb, 1, g_mid)
        load(1, 0).start()
        load(2, 1).start()
        load(1, 0).wait()
        load(2, 1).wait()
        relay.taker()
        wide_dot(total, 0, k_mid)
        wide_dot(total, 1, v_mid)

        def both(rows, cols, key_ok):
            ctx, gq, gk, gv = gradients(
                q_mid[rows, cols], k_mid[rows, cols], v_mid[rows, cols], g_mid[rows, cols], key_ok, True
            )
            ctx_ref[rows, cols], gq_ref[rows, cols], gk_ref[rows, cols], gv_ref[rows, cols] = ctx, gq, gk, gv

        each_head(both)
        send_terms(lambda index: dot_nt(gk_ref[...], block(0, index)) + dot_nt(gv_ref[...], block(1, index)))
        gather.open()
        relay.sender(False)
        slot_b.middle()
        slot_a.third()
        gather.middle(0)
        slot_a.close()
        grams(xa, gram_a)
        grams(xb, gram_b)

        def value_of(e):
            rows = total[pl.ds(e * 128, 128)]
            return (
                gram_a[e] * thin_gram(gq_ref, e)
                + dot_nt(rows, rows) * (thin_gram(gk_ref, e) + thin_gram(gv_ref, e))
                + gram_b[e] * thin_gram(ctx_ref, e)
            )

        note(value_of)
        slot_b.second()
        gather.close()
        slot_b.third()
        slot_b.close()
        relay.sender_close()
        relay.gather.close()


def bridge(lens, q, k, v, rows_in, xa, cot, mats):
    thin = jax.ShapeDtypeStruct((ROWS, PIECE), BF16)
    small = pltpu.VMEM((ROWS, PIECE), BF16)
    square = pltpu.VMEM((2, 128, 128), F32)
    return pl.pallas_call(
        bridge_kernel,
        name="bridge",
        out_shape=(thin,) * 4
        + (
            jax.ShapeDtypeStruct((ROWS, D), BF16),
            jax.ShapeDtypeStruct((8, 128), F32),
            jax.ShapeDtypeStruct((4, N * ROWS, PIECE), BF16),
            jax.ShapeDtypeStruct((3, N * ROWS, PIECE), BF16),
        ),
        in_specs=[SM] + [VM] * 3 + [HBM, VM, VM, HBM],
        out_specs=(VM,) * 6 + (HBM, HBM),
        scratch_shapes=RELAY_BUFS
        + RELAY_SEMS
        + [
            DMA((1, 8)),
            DMA((1, 8)),
            DMA((1,)),
            DMA((2,)),
            pltpu.VMEM((2, D, PIECE), BF16),
            pltpu.VMEM((ROWS, D), BF16),
            small,
            small,
            small,
            small,
            square,
            square,
            pltpu.VMEM((ROWS, D), BF16),
            small,
            DMA,
            pltpu.VMEM((2, ROWS, PIECE), BF16),
            DMA((2,)),
            DMA((2,)),
            DMA((2,)),
            DMA((2, SLICE_CHUNKS, 7)),
            DMA((2, SLICE_CHUNKS, 7)),
            DMA((2, SLICE_CHUNKS)),
        ],
        compiler_params=pltpu.CompilerParams(collective_id=1, has_side_effects=True),
    )(lens, q, k, v, rows_in, xa, cot, mats)


def final_kernel(
    gq, gk, gv, relayed, norm, slices_in, rights_in, slices, rights, norms,
    turn, norm_mp, norm_own, norm_far, norm_dp,
    y_send, y_recv, y_loc, t_send, t_recv, t_loc, b_send, b_recv, b_loc, n_send, n_recv, f_send, f_recv, e_send, e_recv,
):
    s, d, m = coords()
    dp_all = [(s, (d + i) % N, m) for i in range(1, N)]
    greet(mp_peers(s, d, m) + dp_all + [(1 - s, d, m)], (d != m, (s, m, d)))
    parts = (gq, gk, gv)
    gather = DpGather(
        3,
        lambda j: parts[j],
        lambda j, b: rights.at[j, pl.ds(pl.multiple_of(b * ROWS, ROWS), ROWS)],
        lambda j, b, h: rights.at[j, pl.ds(pl.multiple_of(b * ROWS + h * 128, 128), 128)],
        y_send,
        y_recv,
        y_loc,
    )
    slot = SliceGather(
        piece(relayed, m), turn, slices.at[2], t_send, t_recv, t_loc, b_send, b_recv, b_loc
    )

    def to_mp(i):
        return rc(norm, norm_mp.at[m], n_send.at[i - 1], n_recv.at[i - 1], (s, d, (m + i) % N))

    def from_mp(i):
        ref = norm_mp.at[(m + N - i) % N]
        return rc(ref, ref, n_send.at[i - 1], n_recv.at[i - 1], (s, d, (m + i) % N))

    def to_dp(i):
        return rc(norm_dp, norms.at[d], e_send.at[i - 1], e_recv.at[i - 1], (s, (d + i) % N, m))

    def from_dp(i):
        ref = norms.at[(d + N - i) % N]
        return rc(ref, ref, e_send.at[i - 1], e_recv.at[i - 1], (s, (d + i) % N, m))

    slot.open()
    for i in range(1, N):
        to_mp(i).start()
    gather.open()
    norm_mp[m] = norm[...]
    for i in range(1, N):
        from_mp(i).wait_recv()
    acc = norm_mp[0]
    for i in range(1, N):
        acc = acc + norm_mp[i]
    norm_own[...] = acc
    over = rc(norm_own, norm_far, f_send, f_recv, (1 - s, d, m))
    over.start()
    slot.middle()
    gather.middle(0)
    slot.second()
    over.wait_recv()
    both = norm_own[...] + norm_far[...]
    norm_dp[...] = both
    norms[d] = both
    for i in range(1, N):
        to_dp(i).start()
    slot.third()
    gather.middle(1)
    gather.middle(2)
    gather.close()
    slot.close()
    for i in range(1, N):
        from_dp(i).wait_recv()
    for i in range(1, N):
        to_mp(i).wait_send()
        to_dp(i).wait_send()
    over.wait_send()


def gather_grads(gq, gk, gv, relayed, norm, slices, rights):
    small = pltpu.VMEM((8, 128), F32)
    return pl.pallas_call(
        final_kernel,
        name="gather_grads",
        out_shape=(
            jax.ShapeDtypeStruct(slices.shape, BF16),
            jax.ShapeDtypeStruct(rights.shape, BF16),
            jax.ShapeDtypeStruct((N, 8, 128), F32),
        ),
        in_specs=[VM, VM, VM, ANY, VM, HBM, HBM],
        out_specs=(HBM, HBM, VM),
        scratch_shapes=[
            pltpu.VMEM((ROWS, PIECE), BF16),
            pltpu.VMEM((N, 8, 128), F32),
            small,
            small,
            small,
            DMA((3, 8)),
            DMA((3, 8)),
            DMA((3,)),
            DMA,
            DMA,
            DMA,
            DMA((SLICE_CHUNKS, 7)),
            DMA((SLICE_CHUNKS, 7)),
            DMA((SLICE_CHUNKS,)),
            DMA((7,)),
            DMA((7,)),
            DMA,
            DMA,
            DMA((7,)),
            DMA((7,)),
        ],
        input_output_aliases={5: 0, 6: 1},
        compiler_params=pltpu.CompilerParams(collective_id=3, has_side_effects=True),
    )(gq, gk, gv, relayed, norm, slices, rights)


def dot_nt(a, b):
    return lax.dot_general(a, b, (((1,), (1,)), ((), ())), preferred_element_type=F32)


def dot_nn(a, b):
    return lax.dot_general(a, b, (((1,), (0,)), ((), ())), preferred_element_type=F32)


def dot_tn(a, b):
    return lax.dot_general(a, b, (((0,), (0,)), ((), ())), preferred_element_type=F32)


def head_masks():
    lane = lax.broadcasted_iota(jnp.int32, (128, 128), 1)
    return lane < HEAD, lane >= HEAD


def soft(q, k, mask, key_ok):
    zero = jnp.zeros_like(q)
    scores = dot_nt(jnp.where(mask, q, zero), k) * HEAD ** (-0.5)
    scores = jnp.where(key_ok, scores, -jnp.inf)
    weights = jnp.exp(scores - jnp.max(scores, axis=-1, keepdims=True))
    return weights / jnp.sum(weights, axis=-1, keepdims=True)


def context(q, k, v, key_ok):
    zero = jnp.zeros_like(q)
    ctx = jnp.zeros((128, 128), F32)
    for mask in head_masks():
        probs = soft(q, k, mask, key_ok)
        ctx = ctx + dot_nn(probs.astype(BF16), jnp.where(mask, v, zero))
    return ctx.astype(BF16)


def gradients(q, k, v, g, key_ok, with_context):
    zero = jnp.zeros_like(q)
    ctx = gq = gk = gv = jnp.zeros((128, 128), F32)
    for mask in head_masks():
        probs = soft(q, k, mask, key_ok)
        low = probs.astype(BF16)
        g_one = jnp.where(mask, g, zero)
        gp = dot_nt(g_one, v)
        inner = jnp.sum(gp * probs, axis=-1, keepdims=True)
        gs = (probs * (gp - inner) * HEAD ** (-0.5)).astype(BF16)
        if with_context:
            ctx = ctx + dot_nn(low, jnp.where(mask, v, zero))
        gq = gq + dot_nn(gs, jnp.where(mask, k, zero))
        gk = gk + dot_tn(gs, jnp.where(mask, q, zero))
        gv = gv + dot_tn(low, g_one)
    return tuple(value.astype(BF16) for value in (ctx, gq, gk, gv))


BLOCK = 128


def weight_kernel(sec, clip, x_ref, y_ref, noise_ref, out_ref, scaled):
    @pl.when(pl.program_id(0) == 0)
    def _():
        for mat in range(4):

            @pl.loop(0, 16)
            def _(e):
                rows = pl.ds(pl.multiple_of(e * 128, 128), 128)
                scaled[mat, rows] = (y_ref[mat, rows].astype(F32) * clip[e]).astype(BF16)

    is_dec = sec[0]
    picks = (0, 2 * is_dec, 2 * is_dec, 2 - is_dec)
    for mat in range(4):
        total = dot_tn(x_ref[picks[mat]], scaled[mat])
        out_ref[:, mat, :] = (total + noise_ref[:, mat, :]) * (1.0 / 16.0)


def weight_grads(sec, clip, slices, rights, dp_noise):
    wide = pl.BlockSpec((BLOCK, 4, PIECE), lambda b: (b, 0, 0))
    return pl.pallas_call(
        weight_kernel,
        name="weight_grads",
        grid=(PIECE // BLOCK,),
        in_specs=[
            SM,
            SM,
            pl.BlockSpec((3, N * ROWS, BLOCK), lambda b: (0, 0, b)),
            pl.BlockSpec((4, N * ROWS, PIECE), lambda b: (0, 0, 0), pipeline_mode=pl.Buffered(1)),
            wide,
        ],
        out_specs=wide,
        out_shape=jax.ShapeDtypeStruct((PIECE, 4, PIECE), F32),
        scratch_shapes=[pltpu.VMEM((4, N * ROWS, PIECE), BF16)],
    )(sec, clip, slices, rights, dp_noise)


def per_device(inputs, norm_gains, weights, cotangent, lengths, dp_noise):
    sec = jnp.reshape(lax.axis_index("section"), (1,)).astype(jnp.int32)
    rows_in = inputs[0].reshape(ROWS, D)
    wt = jnp.swapaxes(weights[0], 0, 1)
    full, normed, q, k, v = gather_weights(wt, rows_in, norm_gains)
    mats = full.reshape(4, D, PIECE)
    ctx, gq, gk, gv, relayed, norm, rights, slices = bridge(
        lengths, q, k, v, rows_in, normed, cotangent.reshape(ROWS, D), mats
    )
    slices, rights, norms = gather_grads(gq, gk, gv, relayed, norm, slices, rights)
    sq_norm = norms[:, 0, :2]
    bound = jnp.sqrt(jnp.float32(8.0 * D * HEADS * HEAD))
    clip_all = bound / (jnp.sqrt(sq_norm) + 0.01 * bound)
    clip_scale = lax.dynamic_index_in_dim(clip_all, lax.axis_index("dp"), 0, keepdims=False)
    noisy_grad = weight_grads(sec, clip_all.reshape(16), slices, rights, dp_noise[0])
    return (noisy_grad[None], clip_scale)


def solution(mesh):
    placed = (
        P("section", "dp", None, None),
        P("section", None),
        P("section", "dp", None, "mp"),
        P("dp", None, None),
        P(None, "dp"),
        P("section", "dp", None, "mp"),
    )
    return jax.shard_map(
        per_device,
        mesh=mesh,
        in_specs=placed,
        out_specs=(P("section", "dp", None, "mp"), P("dp")),
        check_vma=False,
    )
```
